512 devices in a mesh: mapx: 32 (over x, z), mapy: 8 (over y), layer: 2 (over core).
Axes of the slice: x: 4, y: 8, z: 8, core: 2. Of those that a mesh axis runs over, the one named last changes fastest.
Arguments:
- old_state: float32 [32, 8, 2, 6, 8192], P('mapx', 'mapy', 'layer'), as said below
- send_blocks: int32 [32, 8, 2, 10, 16], P('mapx', 'mapy', 'layer'), may hold values from 0 to 63
- node_slots: int32 [32, 8, 2, 4, 512], P('mapx', 'mapy', 'layer'), may hold values from 0 to 20479, as said below
- node_weights: float32 [32, 8, 2, 4, 512], P('mapx', 'mapy', 'layer'), as said below
- front_mask: int32 [32, 8, 2, 512], P('mapx', 'mapy', 'layer'), may hold values 0 or 1
- halo_lists: int32 [32, 8, 2, 6, 256], P('mapx', 'mapy', 'layer'), may hold values from 0 to 511
- elem_nodes: int32 [32, 8, 2, 4, 2560], P('mapx', 'mapy', 'layer'), may hold values from 0 to 2047
- shape_grads: float32 [32, 8, 2, 12, 2560], P('mapx', 'mapy', 'layer'), as said below
- elem_volume: float32 [32, 8, 2, 2560], P('mapx', 'mapy', 'layer'), may hold values from 0.5 to 2
Outputs:
- new_state: float32 [32, 8, 2, 6, 512], P('mapx', 'mapy', 'layer')
- residual: float32 [32, 8, 2, 4, 512], P('mapx', 'mapy', 'layer')
The draws below stay inside these ranges and needn't reach their ends.
Inputs may be any that keep to these rules, and one draw needn't show every extreme that they name: `send_blocks`: each entry names one of the sender's old blocks; a block may go to several peers or twice to one. `node_slots`: indexes the received nodes, ordered by source (mapx offset plus 2, times 2, plus layer index), then slot, then node in the block; only sources inside the device grid are named. `node_weights`: Positive; the four weights of a node sum to one. `halo_lists`: owned nodes kept as ghosts by the neighbour in direction k. `elem_nodes`: local numbering: the owned nodes first, then 256 ghosts for each of the six directions in order. `shape_grads`: the four gradients of an element sum to zero. `old_state`: rows 0 to 3 velocity and pressure, row 4 temperature in [-1, 0], row 5 damage in [0, 0.9].
All inputs are finite; a program needn't handle non-finite values. No bound on the sum of `front_mask` on one device may be relied on, other than what follows from the above.
Results may differ from the reference program's by a relative error of at most 0.00002.
Values sent between devices are 32-bit elements; how exact they have to be, the bound alone decides.
A program may use at most 64 MiB of HBM per device.

```python
import math
import jax
import jax.numpy as jnp
from jax import lax

BLOCK = 128
REACH = 2
OLD_BLK = 64
CAP_PEER = 16
HALO = 256
OLD_NODES = 8192
NEW_NODES = 512
ELEMS = 2560
PEERS = 10
N_MAPX = 32
N_MAPY = 8
N_LAYER = 2


def draw_old_state(key, part):
    first, second, third = jax.random.split(key, 3)
    dims_flow = (N_MAPX, N_MAPY, N_LAYER, 4, OLD_NODES)
    dims_one = (N_MAPX, N_MAPY, N_LAYER, 1, OLD_NODES)
    flow = jax.random.normal(first, dims_flow, jnp.float32)
    temper = jax.random.uniform(second, dims_one, jnp.float32, -1.0, 0.0)
    damage = jax.random.uniform(third, dims_one, jnp.float32, 0.0, 0.9)
    return jnp.concatenate([flow, temper, damage], axis=3)


def draw_node_slots(key, part):
    first, second, third, fourth = jax.random.split(jax.random.fold_in(key, 7), 4)
    dims_all = (N_MAPX, N_MAPY, N_LAYER, 4, NEW_NODES)
    column = jnp.arange(N_MAPX, dtype=jnp.int32).reshape(N_MAPX, 1, 1, 1, 1)
    lowest = jnp.maximum(-REACH, -column)
    highest = jnp.minimum(REACH, N_MAPX - 1 - column)
    lowest = jnp.broadcast_to(lowest, dims_all)
    highest = jnp.broadcast_to(highest, dims_all)
    offset = jax.random.randint(first, dims_all, lowest, highest + 1)
    source_layer = jax.random.randint(second, dims_all, 0, N_LAYER)
    slot = jax.random.randint(third, dims_all, 0, CAP_PEER)
    within = jax.random.randint(fourth, dims_all, 0, BLOCK)
    return ((((offset + REACH) * N_LAYER + source_layer) * CAP_PEER + slot) * BLOCK + within).astype(jnp.int32)


def draw_node_weights(key, part):
    dims_all = (N_MAPX, N_MAPY, N_LAYER, 4, NEW_NODES)
    raw = jax.random.uniform(key, dims_all, jnp.float32, 0.2, 1.0)
    return raw / jnp.sum(raw, axis=3, keepdims=True)


def draw_shape_grads(key, part):
    dims_three = (N_MAPX, N_MAPY, N_LAYER, 3, 3, ELEMS)
    three = jax.random.normal(key, dims_three, jnp.float32)
    fourth = -(three[:, :, :, 0:1] + three[:, :, :, 1:2] + three[:, :, :, 2:3])
    return jnp.concatenate([three, fourth], axis=3).reshape(N_MAPX, N_MAPY, N_LAYER, 12, ELEMS)


def touch_ends(values, own_key, smallest, top_value):
    shape = values.shape
    spot = [jax.random.randint(jax.random.fold_in(own_key, axis), (), 0, shape[axis]) for axis in range(len(shape))]
    values = values.at[tuple(spot)].set(smallest)
    longest = shape.index(max(shape))
    spot[longest] = (spot[longest] + 1) % shape[longest]
    return values.at[tuple(spot)].set(top_value)


def shard_levels(rng, dims, cuts, least, largest):
    factor_of, own = 1.0, jax.random.fold_in(rng, 6)
    for axis_at, parts in cuts:
        heights = jnp.exp(jax.random.uniform(jax.random.fold_in(own, axis_at), (parts,), jnp.float32, least / len(cuts), largest / len(cuts)))
        factor_of = factor_of * jnp.repeat(heights, dims[axis_at] // parts).reshape([-1 if axis == axis_at else 1 for axis in range(len(dims))])
    return factor_of


def setup_inputs(seed: int = 0) -> dict:
    key_of = jax.random.split(jax.random.key(seed), 10)
    old_state = draw_old_state(jax.random.fold_in(key_of[9], 71), 0)
    send_blocks = touch_ends(jax.random.randint(key_of[1], (N_MAPX, N_MAPY, N_LAYER, PEERS, CAP_PEER), 0, OLD_BLK), jax.random.fold_in(key_of[1], 1), 0, OLD_BLK - 1).astype(jnp.int32)
    node_slots = draw_node_slots(jax.random.fold_in(key_of[9], 71), 0)
    node_weights = draw_node_weights(jax.random.fold_in(key_of[9], 71), 0)
    front_mask = touch_ends((jax.random.randint(key_of[4], (N_MAPX, N_MAPY, N_LAYER, NEW_NODES), 0, 8) < 1).astype(jnp.int32), jax.random.fold_in(key_of[4], 1), 0, 1)
    halo_lists = touch_ends(jax.random.randint(key_of[5], (N_MAPX, N_MAPY, N_LAYER, 6, HALO), 0, NEW_NODES), jax.random.fold_in(key_of[5], 1), 0, NEW_NODES - 1).astype(jnp.int32)
    elem_nodes = touch_ends(jax.random.randint(key_of[6], (N_MAPX, N_MAPY, N_LAYER, 4, ELEMS), 0, NEW_NODES + 6 * HALO), jax.random.fold_in(key_of[6], 1), 0, (NEW_NODES + 6 * HALO) - 1).astype(jnp.int32)
    shape_grads = draw_shape_grads(jax.random.fold_in(key_of[9], 71), 0)
    elem_volume = jnp.clip(jnp.exp(math.log(2.0) - 1.3862944 * jax.random.uniform(key_of[8], (N_MAPX, N_MAPY, N_LAYER, ELEMS), jnp.float32) ** shard_levels(key_of[8], (N_MAPX, N_MAPY, N_LAYER, ELEMS), ((0, 32), (1, 8), (2, 2)), -0.2, 0.2)), 0.5, 2.0)
    return dict(old_state=old_state, send_blocks=send_blocks, node_slots=node_slots, node_weights=node_weights, front_mask=front_mask, halo_lists=halo_lists, elem_nodes=elem_nodes, shape_grads=shape_grads, elem_volume=elem_volume)


ocean_temp = 0.0
strain_reg = 0.01
gravity = 0.5


def element_residual(node_table, elem_nodes, shape_grads, elem_volume):
    values = jnp.take(node_table, elem_nodes, axis=1)
    grads = shape_grads.reshape(4, 3, -1)
    velgrad = jnp.sum(values[:3, :, None, :] * grads[None, :, :, :], axis=1)
    strain = 0.5 * (velgrad + jnp.transpose(velgrad, (1, 0, 2)))
    second = 0.5 * jnp.sum(strain * strain, axis=(0, 1))
    means = jnp.mean(values[3:], axis=1)
    viscosity = 0.5 * (1.0 - means[2]) * jnp.exp(-means[1]) * (second + strain_reg) ** (-1.0 / 3.0)
    stress = 2.0 * viscosity * strain - means[0] * jnp.eye(3, dtype=strain.dtype)[:, :, None]
    momentum = elem_volume * jnp.sum(stress[None, :, :, :] * grads[:, None, :, :], axis=2)
    upward = jnp.array([0.0, 0.0, 1.0], dtype=momentum.dtype)
    momentum = momentum + (0.25 * gravity * elem_volume)[None, None, :] * upward[None, :, None]
    divergence = velgrad[0, 0] + velgrad[1, 1] + velgrad[2, 2]
    continuity = 0.25 * elem_volume * divergence
    cont_rows = jnp.broadcast_to(continuity[None, None, :], (4, 1, continuity.shape[0]))
    return jnp.concatenate([momentum, cont_rows], axis=1)


def assemble(contrib, elem_nodes, width):
    total = jnp.zeros((4, width), contrib.dtype)
    for corner in range(4):
        total = total.at[:, elem_nodes[corner]].add(contrib[corner])
    return total


def shift_grid(grid, dim, step):
    extent = grid.shape[dim]
    zero_part = jnp.zeros_like(lax.slice_in_dim(grid, 0, 1, axis=dim))
    if step > 0:
        return jnp.concatenate([zero_part, lax.slice_in_dim(grid, 0, extent - 1, axis=dim)], axis=dim)
    return jnp.concatenate([lax.slice_in_dim(grid, 1, extent, axis=dim), zero_part], axis=dim)


def pull_columns(grid, offset):
    extent = grid.shape[0]
    if offset == 0:
        return grid
    if offset > 0:
        zero_part = jnp.zeros_like(grid[:offset])
        return jnp.concatenate([grid[offset:], zero_part], axis=0)
    zero_part = jnp.zeros_like(grid[:(-offset)])
    return jnp.concatenate([zero_part, grid[:extent + offset]], axis=0)


def take_cols(table, picks):
    return jnp.take(table, picks, axis=1)


def add_cols(target, picks, addend):
    return target.at[:, picks].add(addend)


def interpolate(table, slot_ids, weights):
    return jnp.sum(jnp.take(table, slot_ids, axis=1) * weights[None], axis=1)


def reference(old_state, send_blocks, node_slots, node_weights, front_mask, halo_lists, elem_nodes, shape_grads, elem_volume):
    devices = N_MAPX * N_MAPY * N_LAYER
    spread = 2 * REACH + 1
    directions = [(0, 1), (0, -1), (1, 1), (1, -1), (2, 1), (2, -1)]
    blocks = old_state.reshape(devices, 6, OLD_BLK, BLOCK)
    picks = send_blocks.reshape(devices, PEERS, CAP_PEER)
    outgoing = jax.vmap(take_cols)(blocks, picks)
    outgoing = outgoing.reshape(N_MAPX, N_MAPY, N_LAYER, 6, spread, N_LAYER, CAP_PEER, BLOCK)
    columns = []
    for source in range(spread):
        offset = source - REACH
        slab = outgoing[:, :, :, :, spread - 1 - source]
        slab = pull_columns(slab, offset)
        columns.append(jnp.transpose(slab, (0, 1, 4, 3, 2, 5, 6)))
    received = jnp.stack(columns, axis=4).reshape(devices, 6, PEERS * CAP_PEER * BLOCK)
    slot_ids = node_slots.reshape(devices, 4, NEW_NODES)
    weights = node_weights.reshape(devices, 4, NEW_NODES)
    interpolated = jax.vmap(interpolate)(received, slot_ids, weights)
    temp_row = (jnp.arange(6) == 4)[None, :, None]
    front = (front_mask.reshape(devices, NEW_NODES) == 1)[:, None, :]
    new_state = jnp.where(temp_row & front, ocean_temp, interpolated)
    halos = halo_lists.reshape(devices, 6, HALO)
    pieces = [new_state]
    for index in range(6):
        dim, step = directions[index]
        portion = jax.vmap(take_cols)(new_state, halos[:, index])
        grid = portion.reshape(N_MAPX, N_MAPY, N_LAYER, 6, HALO)
        pieces.append(shift_grid(grid, dim, step).reshape(devices, 6, HALO))
    node_table = jnp.concatenate(pieces, axis=2)
    width = NEW_NODES + 6 * HALO

    def device_residual(inputs):
        table, nodes, grads, volume = inputs
        contrib = element_residual(table, nodes, grads, volume)
        return assemble(contrib, nodes, width)

    assembled = lax.map(device_residual, (node_table, elem_nodes.reshape(devices, 4, ELEMS), shape_grads.reshape(devices, 12, ELEMS), elem_volume.reshape(devices, ELEMS)))
    residual = assembled[:, :, :NEW_NODES]
    for index in range(6):
        dim, step = directions[index]
        start = NEW_NODES + index * HALO
        portion = assembled[:, :, start:start + HALO]
        grid = portion.reshape(N_MAPX, N_MAPY, N_LAYER, 4, HALO)
        arrived = shift_grid(grid, dim, -step).reshape(devices, 4, HALO)
        residual = jax.vmap(add_cols)(residual, halos[:, index], arrived)
    return (new_state.reshape(N_MAPX, N_MAPY, N_LAYER, 6, NEW_NODES), residual.reshape(N_MAPX, N_MAPY, N_LAYER, 4, NEW_NODES))
```

```python
import functools

import jax
import jax.numpy as jnp
from jax import lax
from jax.experimental import pallas as pl
from jax.experimental.pallas import tpu as pltpu
from jax.sharding import PartitionSpec as P

MESH = pl.DeviceIdType.MESH
F32 = jnp.float32
BF16 = jnp.bfloat16
LANES = 128
FIELDS = 6
ROWS = 4
SIDES = 5
SPOTS = 80
CAP = 16

ocean_temp = 0.0
strain_reg = 0.01
gravity = 0.5


def lane_gather(row, lanes):
    return jnp.take_along_axis(row, lanes, axis=1)


def split_two(value):
    high = value.astype(BF16).astype(F32)
    return high, value - high


def kernel(
    count_x,
    count_y,
    blocks,
    old,
    slots,
    weights,
    front,
    halos,
    nodes,
    grads,
    volume,
    out_new,
    out_res,
    req_slots,
    req_weights,
    part_out,
    part_in,
    state,
    pairs,
    halo_idx,
    halo_out,
    ghost_in,
    spot_idx,
    values,
    vol_rows,
    contrib,
    left,
    right,
    ret_out,
    ret_in,
    own_sum,
    req_send,
    req_recv,
    part_send,
    part_recv,
    halo_send,
    halo_recv,
    ret_send,
    ret_recv,
):
    x = lax.axis_index("mapx")
    y = lax.axis_index("mapy")
    layer = lax.axis_index("layer")

    def device(dx, dy, which):
        return (lax.rem(x + dx + count_x, count_x), lax.rem(y + dy + count_y, count_y), which)

    far = [(t, lp) for t in (-2, 2, -1, 1) for lp in (0, 1)]
    peers = [((t + 2) * 2 + lp, (2 - t) * 2 + layer, device(t, 0, lp)) for t, lp in far]
    peers.append((4 + (1 - layer), 4 + layer, device(0, 0, 1 - layer)))
    sides = [device(1, 0, layer), device(-1, 0, layer), device(0, 1, layer), device(0, -1, layer), device(0, 0, 1 - layer)]
    backs = [sides[1], sides[0], sides[3], sides[2], sides[4]]

    barrier = pltpu.get_barrier_semaphore()
    greet = [peer[2] for peer in peers] + [sides[2], sides[3]]
    for other in greet:
        pl.semaphore_signal(barrier, inc=1, device_id=other, device_id_type=MESH)

    me = 4 + layer
    for j in range(ROWS):
        req_slots[10, pl.ds(j, 4, stride=4), :] = slots[:, j * LANES : (j + 1) * LANES]
        req_weights[10, pl.ds(j, 4, stride=4), :] = weights[:, j * LANES : (j + 1) * LANES]
    pl.semaphore_wait(barrier, len(greet))

    def request(number, theirs, other):
        return [
            pltpu.make_async_remote_copy(
                src_ref=ref.at[10],
                dst_ref=ref.at[theirs],
                send_sem=req_send.at[which, number],
                recv_sem=req_recv.at[which, theirs],
                device_id=other,
                device_id_type=MESH,
            )
            for which, ref in enumerate((req_slots, req_weights))
        ]

    def request_in(number, other):
        for which, ref in enumerate((req_slots, req_weights)):
            pltpu.make_async_remote_copy(
                src_ref=ref.at[10],
                dst_ref=ref.at[number],
                send_sem=req_send.at[which, number],
                recv_sem=req_recv.at[which, number],
                device_id=other,
                device_id_type=MESH,
            ).wait_recv()

    for peer in peers:
        for copy in request(*peer):
            copy.start()

    def partial(spot, number, theirs, dest):
        lo, blk, wgt = [], [], []
        for v in range(2):
            s = req_slots[spot, v * 8 : (v + 1) * 8, :]
            lo.append(jnp.bitwise_and(s, LANES - 1))
            blk.append(jnp.right_shift(s, 7) - theirs * CAP)
            wgt.append(req_weights[spot, v * 8 : (v + 1) * 8, :])

        def step(c, acc):
            b = blocks[number, c]
            hit = [blk[v] == c for v in range(2)]
            new = []
            for f in range(FIELDS):
                row = jnp.broadcast_to(old[f, pl.ds(b, 1), :], (8, LANES))
                for v in range(2):
                    new.append(jnp.where(hit[v], lane_gather(row, lo[v]), acc[f * 2 + v]))
            return tuple(new)

        acc = lax.fori_loop(0, CAP, step, tuple(jnp.zeros((8, LANES), F32) for _ in range(12)), unroll=2)
        for f in range(FIELDS):
            both = acc[f * 2] * wgt[0] + acc[f * 2 + 1] * wgt[1]
            part_out[dest, f * 4 : (f + 1) * 4, :] = both[0:4] + both[4:8]

    def send_part(number, theirs, other):
        return pltpu.make_async_remote_copy(
            src_ref=part_out.at[number],
            dst_ref=part_in.at[theirs],
            send_sem=part_send.at[number],
            recv_sem=part_recv.at[theirs],
            device_id=other,
            device_id_type=MESH,
        )

    partial(10, me, me, 10)

    for j in range(20):
        spot_idx[j * 4 : (j + 1) * 4, :] = nodes[:, j * LANES : (j + 1) * LANES]
    for j in range(5):
        vol_rows[j * 4 : (j + 1) * 4, :] = volume[j]
    for k in range(SIDES):
        pair = halos[k] if k < 4 else halos[4 + layer]
        for d in range(4):
            halo_idx[k, d * 2 : (d + 1) * 2, :] = pair

    for number, theirs, other in [peers[8]] + peers[:8]:
        request_in(number, other)
        partial(number, number, theirs, number)
        send_part(number, theirs, other).start()

    total = part_out[10]
    for number, theirs, other in [peers[8]] + peers[:8]:
        pltpu.make_async_remote_copy(
            src_ref=part_out.at[number],
            dst_ref=part_in.at[number],
            send_sem=part_send.at[number],
            recv_sem=part_recv.at[number],
            device_id=other,
            device_id_type=MESH,
        ).wait_recv()
        total = total + part_in[number]
    state[...] = total
    state[16:20, :] = jnp.where(front[...] == 1, ocean_temp, state[16:20, :])

    for h in range(ROWS):
        for f in range(8):
            src = f if f < FIELDS else f - 2
            pairs[h, f * 2 : (f + 1) * 2, :] = jnp.broadcast_to(state[pl.ds(src * 4 + h, 1), :], (2, LANES))

    def halo_copy(k):
        return pltpu.make_async_remote_copy(
            src_ref=halo_out.at[k],
            dst_ref=ghost_in.at[k],
            send_sem=halo_send.at[k],
            recv_sem=halo_recv.at[k],
            device_id=sides[k],
            device_id_type=MESH,
        )

    for k in range(SIDES):
        idx = halo_idx[k]
        lo = jnp.bitwise_and(idx, LANES - 1)
        hi = jnp.right_shift(idx, 7)
        for g in range(2):
            acc = jnp.zeros((8, LANES), F32)
            for h in range(ROWS):
                acc = jnp.where(hi == h, lane_gather(pairs[h, g * 8 : (g + 1) * 8, :], lo), acc)
            halo_out[k, g * 8 : (g + 1) * 8, :] = acc
        halo_copy(k).start()

    for f in range(FIELDS):
        out_new[f] = state[f * 4 : (f + 1) * 4, :]

    def gather_rows(t, table, first):
        at = pl.ds(pl.multiple_of(t * 8, 8), 8)
        idx = spot_idx[at, :]
        lo = jnp.bitwise_and(idx, LANES - 1)
        hi = jnp.right_shift(idx, 7)
        acc = [jnp.zeros((8, LANES), F32) if first else values[f, at, :] for f in range(FIELDS)]
        for code, fetch in table:
            hit = hi == code
            for f in range(FIELDS):
                row = jnp.broadcast_to(fetch(f), (8, LANES))
                acc[f] = jnp.where(hit, lane_gather(row, lo), acc[f])
        for f in range(FIELDS):
            values[f, at, :] = acc[f]

    own_table = [(h, lambda f, h=h: state[f * 4 + h : f * 4 + h + 1, :]) for h in range(ROWS)]
    lax.fori_loop(0, SPOTS // 8, lambda t, c: (gather_rows(t, own_table, True), c)[1], 0)

    low_x, high_x = x > 0, x < count_x - 1
    low_y, high_y = y > 0, y < count_y - 1
    ghost_live = [low_x, high_x, low_y, high_y]
    back_live = [high_x, low_x, high_y, low_y]
    ghost_table = []
    for k in range(SIDES):
        for r in range(2):
            code = jnp.where(ghost_live[k], 4 + 2 * k + r, -1) if k < 4 else 4 + 2 * (5 - layer) + r
            ghost_table.append((code, lambda f, k=k, r=r: ghost_in[k, f * 2 + r : f * 2 + r + 1, :]))
    for k in range(SIDES):
        halo_copy(k).wait_recv()
    lax.fori_loop(0, SPOTS // 8, lambda t, c: (gather_rows(t, ghost_table, False), c)[1], 0)

    for r0 in (0, 8, 12):
        val = [[values[f, pl.ds(r0 * 4 + a, 8, stride=4), :] for a in range(4)] for f in range(FIELDS)]
        grad = [[grads[(3 * a + j) * 20 + r0 : (3 * a + j) * 20 + r0 + 8, :] for j in range(3)] for a in range(4)]
        vol = vol_rows[r0 : r0 + 8, :]
        vg = [[sum(val[i][a] * grad[a][j] for a in range(4)) for j in range(3)] for i in range(3)]
        strain = [[0.5 * (vg[i][j] + vg[j][i]) for j in range(3)] for i in range(3)]
        second = 0.5 * sum(strain[i][j] * strain[i][j] for i in range(3) for j in range(3))
        pm, tm, dm = [0.25 * (val[f][0] + val[f][1] + val[f][2] + val[f][3]) for f in (3, 4, 5)]
        visc2 = (1.0 - dm) * jnp.exp(-tm) * jnp.exp(jnp.log(second + strain_reg) * (-1.0 / 3.0))
        stress = [[visc2 * strain[i][j] - (pm if i == j else 0.0) for j in range(3)] for i in range(3)]
        cont = 0.25 * vol * (vg[0][0] + vg[1][1] + vg[2][2])
        for a in range(4):
            for c in range(4):
                if c < 3:
                    part = vol * sum(stress[c][j] * grad[a][j] for j in range(3))
                    if c == 2:
                        part = part + 0.25 * gravity * vol
                else:
                    part = cont
                for d in range(2):
                    contrib[pl.ds((r0 * 4 + a) * 8 + d * 4 + c, 8, stride=32), :] = part

    sub = lax.broadcasted_iota(jnp.int32, (8, LANES), 0)
    half = jnp.right_shift(sub, 2)

    def one_hot(lo_row, u):
        cols = []
        for g in range(16):
            cols.append(jnp.where(lo_row == sub + g * 8, 1.0, 0.0))
        right[:, u * LANES : (u + 1) * LANES] = jnp.concatenate(cols, axis=0).astype(BF16)

    def chunk(t, acc):
        for u in range(8):
            s = t * 8 + u
            idx = jnp.broadcast_to(spot_idx[pl.ds(s, 1), :], (8, LANES))
            one_hot(jnp.bitwise_and(idx, LANES - 1), u)
            hi = jnp.right_shift(idx, 7) - half
            parts = split_two(contrib[pl.ds(pl.multiple_of(s * 8, 8), 8), :])
            for part in range(2):
                rows = [jnp.where(hi == 2 * m, parts[part], 0.0) for m in range(8)]
                left[part * 64 : (part + 1) * 64, u * LANES : (u + 1) * LANES] = jnp.concatenate(rows, axis=0).astype(BF16)
        return acc + lax.dot_general(left[...], right[...], (((1,), (1,)), ((), ())), preferred_element_type=F32)

    acc = lax.fori_loop(0, SPOTS // 8, chunk, jnp.zeros((128, LANES), F32))
    sums = acc[0:64] + acc[64:128]
    own_sum[...] = sums

    def ret_copy(k):
        return pltpu.make_async_remote_copy(
            src_ref=ret_out.at[k],
            dst_ref=ret_in.at[k],
            send_sem=ret_send.at[k],
            recv_sem=ret_recv.at[k],
            device_id=backs[k],
            device_id_type=MESH,
        )

    for k in range(4):
        ret_out[k] = own_sum[16 + k * 8 : 24 + k * 8, :]
    ret_out[4] = own_sum[pl.ds(pl.multiple_of(16 + (5 - layer) * 8, 8), 8), :]
    for k in range(SIDES):
        ret_copy(k).start()

    final = jnp.zeros((32, LANES), F32)
    for k in range(SIDES):
        for r in range(2):
            u = k * 2 + r
            idx = jnp.broadcast_to(halo_idx[k, r : r + 1, :], (8, LANES))
            one_hot(jnp.bitwise_and(idx, LANES - 1), u % 8) if u < 8 else None
    for k in range(SIDES):
        ret_copy(k).wait_recv()

    def returned(k, r, u):
        idx = jnp.broadcast_to(halo_idx[k, r : r + 1, :], (8, LANES))
        hi = jnp.right_shift(idx, 7) - half
        four = ret_in[k, r * 4 : (r + 1) * 4, :]
        value = jnp.concatenate([four, four], axis=0)
        if k < 4:
            value = jnp.where(back_live[k], value, 0.0)
        parts = split_two(value)
        for part in range(2):
            rows = [jnp.where(hi == 2 * m, parts[part], 0.0) for m in range(2)]
            left[part * 16 : (part + 1) * 16, u * LANES : (u + 1) * LANES] = jnp.concatenate(rows, axis=0).astype(BF16)

    for u in range(8):
        returned(u // 2, u % 2, u)
    final = lax.dot_general(left[0:32, :], right[...], (((1,), (1,)), ((), ())), preferred_element_type=F32)
    for r in range(2):
        idx = jnp.broadcast_to(halo_idx[4, r : r + 1, :], (8, LANES))
        one_hot(jnp.bitwise_and(idx, LANES - 1), r)
        returned(4, r, r)
    final = final + lax.dot_general(
        left[0:32, 0:256], right[:, 0:256], (((1,), (1,)), ((), ())), preferred_element_type=F32
    )
    result = own_sum[0:16, :] + final[0:16] + final[16:32]
    for h in range(ROWS):
        out_res[:, h * LANES : (h + 1) * LANES] = result[h * 4 : (h + 1) * 4]

    for peer in peers:
        for copy in request(*peer):
            copy.wait_send()
        send_part(*peer).wait_send()
    for k in range(SIDES):
        halo_copy(k).wait_send()
        ret_copy(k).wait_send()


def per_device(old_state, send_blocks, node_slots, node_weights, front_mask, halo_lists, elem_nodes, shape_grads, elem_volume):
    count_x = lax.axis_size("mapx")
    count_y = lax.axis_size("mapy")
    vmem = pl.BlockSpec(memory_space=pltpu.VMEM)
    smem = pl.BlockSpec(memory_space=pltpu.SMEM)
    dma = pltpu.SemaphoreType.DMA
    new_state, residual = pl.pallas_call(
        functools.partial(kernel, count_x, count_y),
        out_shape=(
            jax.ShapeDtypeStruct((FIELDS, ROWS, LANES), F32),
            jax.ShapeDtypeStruct((4, ROWS * LANES), F32),
        ),
        in_specs=[smem] + [vmem] * 8,
        out_specs=(vmem, vmem),
        scratch_shapes=[
            pltpu.VMEM((11, 16, LANES), jnp.int32),
            pltpu.VMEM((11, 16, LANES), F32),
            pltpu.VMEM((11, 24, LANES), F32),
            pltpu.VMEM((10, 24, LANES), F32),
            pltpu.VMEM((24, LANES), F32),
            pltpu.VMEM((4, 16, LANES), F32),
            pltpu.VMEM((SIDES, 8, LANES), jnp.int32),
            pltpu.VMEM((SIDES, 16, LANES), F32),
            pltpu.VMEM((SIDES, 16, LANES), F32),
            pltpu.VMEM((SPOTS, LANES), jnp.int32),
            pltpu.VMEM((FIELDS, SPOTS, LANES), F32),
            pltpu.VMEM((24, LANES), F32),
            pltpu.VMEM((SPOTS * 8, LANES), F32),
            pltpu.VMEM((128, 1024), BF16),
            pltpu.VMEM((128, 1024), BF16),
            pltpu.VMEM((SIDES, 8, LANES), F32),
            pltpu.VMEM((SIDES, 8, LANES), F32),
            pltpu.VMEM((64, LANES), F32),
            dma((2, 10)),
            dma((2, 10)),
            dma((10,)),
            dma((10,)),
            dma((SIDES,)),
            dma((SIDES,)),
            dma((SIDES,)),
            dma((SIDES,)),
        ],
        compiler_params=pltpu.CompilerParams(collective_id=0, has_side_effects=True),
        name="remap_residual",
    )(
        send_blocks.reshape(10, CAP),
        old_state.reshape(FIELDS, 64, LANES),
        node_slots.reshape(4, 512),
        node_weights.reshape(4, 512),
        front_mask.reshape(ROWS, LANES),
        halo_lists.reshape(6, 2, LANES),
        elem_nodes.reshape(4, 2560),
        shape_grads.reshape(240, LANES),
        elem_volume.reshape(5, 4, LANES),
    )
    return new_state.reshape(1, 1, 1, FIELDS, 512), residual.reshape(1, 1, 1, 4, 512)


def solution(mesh):
    deep = P("mapx", "mapy", "layer", None, None)
    flat = P("mapx", "mapy", "layer", None)
    return jax.shard_map(
        per_device,
        mesh=mesh,
        in_specs=(deep, deep, deep, deep, flat, deep, deep, deep, flat),
        out_specs=(deep, deep),
        check_vma=False,
    )
```

```python
import functools

import jax
import jax.numpy as jnp
from jax import lax
from jax.experimental import pallas as pl
from jax.experimental.pallas import tpu as pltpu
from jax.sharding import PartitionSpec as P

MESH = pl.DeviceIdType.MESH
F32 = jnp.float32
BF16 = jnp.bfloat16
LANES = 128
WIDE = 256
FIELDS = 6
ROWS = 4
SIDES = 5
SPOTS = 80
CAP = 16

ocean_temp = 0.0
strain_reg = 0.01
gravity = 0.5


def lane_gather(row, lanes):
    return jnp.take_along_axis(row, lanes, axis=1)


def split_two(value):
    high = value.astype(BF16).astype(F32)
    return high, value - high


def lane_tile(s):
    return pl.ds(pl.multiple_of(s * LANES, LANES), LANES)


def kernel(
    count_x,
    count_y,
    blocks_in,
    old_in,
    slots_in,
    weights_in,
    front_in,
    halos_in,
    nodes_in,
    grads_in,
    volume_in,
    out,
    blocks,
    old,
    slots,
    weights,
    front,
    halos,
    nodes,
    grads,
    volume,
    block_out,
    block_in,
    lookup,
    weight_rows,
    state,
    halo_idx,
    halo_out,
    ghost_in,
    spot_idx,
    one_hot,
    halo_hot,
    values,
    vol_rows,
    contrib,
    left,
    left_back,
    sums,
    ret_out,
    ret_in,
    in_sem,
    block_send,
    block_recv,
    halo_send,
    halo_recv,
    ret_send,
    ret_recv,
):
    x = lax.axis_index("mapx")
    y = lax.axis_index("mapy")
    layer = lax.axis_index("layer")

    def device(dx, dy, which):
        return (lax.rem(x + dx + count_x, count_x), lax.rem(y + dy + count_y, count_y), which)

    far = [(t, lp) for t in (-2, 2, -1, 1) for lp in (0, 1)]
    peers = [((t + 2) * 2 + lp, (2 - t) * 2 + layer, device(t, 0, lp)) for t, lp in far]
    peers.append((4 + (1 - layer), 4 + layer, device(0, 0, 1 - layer)))
    sides = [device(1, 0, layer), device(-1, 0, layer), device(0, 1, layer), device(0, -1, layer), device(0, 0, 1 - layer)]
    backs = [sides[1], sides[0], sides[3], sides[2], sides[4]]

    barrier = pltpu.get_barrier_semaphore()
    greet = [peer[2] for peer in peers] + [sides[2], sides[3]]
    for other in greet:
        pl.semaphore_signal(barrier, inc=1, device_id=other, device_id_type=MESH)

    pairs_in = [
        (blocks_in, blocks),
        (old_in, old),
        (nodes_in, nodes),
        (halos_in, halos),
        (slots_in, slots),
        (weights_in, weights),
        (front_in, front),
        (grads_in, grads),
        (volume_in, volume),
    ]
    arrivals = [pltpu.make_async_copy(src, dst, in_sem.at[i]) for i, (src, dst) in enumerate(pairs_in)]
    for copy in arrivals:
        copy.start()

    arrivals[0].wait()
    arrivals[1].wait()
    pl.semaphore_wait(barrier, len(greet))

    def block_copy(number, theirs, other):
        return pltpu.make_async_remote_copy(
            src_ref=block_out.at[number],
            dst_ref=block_in.at[theirs],
            send_sem=block_send.at[number],
            recv_sem=block_recv.at[theirs],
            device_id=other,
            device_id_type=MESH,
        )

    def pack(number):
        for c in range(CAP):
            rows = old[pl.ds(blocks[number, 0, c], FIELDS, stride=64), :]
            block_out[number, c * FIELDS : (c + 1) * FIELDS, :] = rows

    for peer in peers:
        pack(peer[0])
        block_copy(*peer).start()
    me = 4 + layer
    pack(me)

    arrivals[2].wait()
    arrivals[3].wait()
    for j in range(20):
        spot_idx[j * 4 : (j + 1) * 4, :] = nodes[:, j * LANES : (j + 1) * LANES]
    for k in range(SIDES):
        halo_idx[k * 2 : k * 2 + 2, :] = halos[k] if k < 4 else halos[4 + layer]

    sub = lax.broadcasted_iota(jnp.int32, (8, LANES), 0)
    half = jnp.right_shift(sub, 2)

    def hot_tile(row):
        low = jnp.bitwise_and(jnp.broadcast_to(row, (8, LANES)), LANES - 1)
        return jnp.concatenate([jnp.where(low == sub + g * 8, 1.0, 0.0) for g in range(16)], axis=0).astype(BF16)

    def build_hot(s, carry):
        one_hot[:, lane_tile(s)] = hot_tile(spot_idx[pl.ds(s, 1), :])
        return carry

    def build_halo_hot(s, carry):
        halo_hot[:, lane_tile(s)] = hot_tile(halo_idx[pl.ds(s, 1), :])
        return carry

    lax.fori_loop(0, SPOTS, build_hot, 0, unroll=8)
    lax.fori_loop(0, SIDES * 2, build_halo_hot, 0, unroll=10)

    arrivals[4].wait()
    arrivals[5].wait()
    for j in range(ROWS):
        lookup[pl.ds(j, 4, stride=4), :] = slots[:, j * LANES : (j + 1) * LANES]
        weight_rows[pl.ds(j, 4, stride=4), :] = weights[:, j * LANES : (j + 1) * LANES]

    for copy in arrivals[6:]:
        copy.wait()
    for j in range(5):
        vol_rows[j * 4 : (j + 1) * 4, :] = volume[j]

    lo = [jnp.bitwise_and(lookup[v * 8 : (v + 1) * 8, :], LANES - 1) for v in range(2)]
    blk = [jnp.right_shift(lookup[v * 8 : (v + 1) * 8, :], 7) for v in range(2)]

    def interpolate(source, spot, number, acc):
        acc = list(acc)
        for c in range(CAP):
            hit = [blk[v] == number * CAP + c for v in range(2)]
            for f in range(FIELDS):
                row = jnp.broadcast_to(source[spot, c * FIELDS + f : c * FIELDS + f + 1, :], (8, LANES))
                for v in range(2):
                    acc[f * 2 + v] = jnp.where(hit[v], lane_gather(row, lo[v]), acc[f * 2 + v])
        return acc

    acc = tuple(jnp.zeros((8, LANES), F32) for _ in range(12))
    acc = interpolate(block_out, me, me, acc)
    for number, _, other in [peers[i] for i in (8, 4, 5, 6, 7, 0, 1, 2, 3)]:
        pltpu.make_async_remote_copy(
            src_ref=block_out.at[number],
            dst_ref=block_in.at[number],
            send_sem=block_send.at[number],
            recv_sem=block_recv.at[number],
            device_id=other,
            device_id_type=MESH,
        ).wait_recv()
        acc = interpolate(block_in, number, number, acc)

    for f in range(FIELDS):
        both = acc[f * 2] * weight_rows[0:8, :] + acc[f * 2 + 1] * weight_rows[8:16, :]
        total = both[0:4] + both[4:8]
        if f == 4:
            total = jnp.where(front[...] == 1, ocean_temp, total)
        state[f * 4 : (f + 1) * 4, :] = total
    state[24:32, :] = jnp.zeros((8, LANES), F32)
    tiles = [state[pl.ds(h, 8, stride=4), :] for h in range(ROWS)]

    def halo_copy(k):
        return pltpu.make_async_remote_copy(
            src_ref=halo_out.at[k],
            dst_ref=ghost_in.at[k],
            send_sem=halo_send.at[k],
            recv_sem=halo_recv.at[k],
            device_id=sides[k],
            device_id_type=MESH,
        )

    for k in range(SIDES):
        for r in range(2):
            idx = jnp.broadcast_to(halo_idx[k * 2 + r : k * 2 + r + 1, :], (8, LANES))
            low = jnp.bitwise_and(idx, LANES - 1)
            high = jnp.right_shift(idx, 7)
            kept = jnp.zeros((8, LANES), F32)
            for h in range(ROWS):
                kept = jnp.where(high == h, lane_gather(tiles[h], low), kept)
            halo_out[k, :, r * LANES : (r + 1) * LANES] = kept
        halo_copy(k).start()

    out[0:24, :] = state[0:24, :]

    def look_up(rows, first):
        for t in range(SPOTS // 8):
            at = slice(t * 8, (t + 1) * 8)
            low = jnp.bitwise_and(spot_idx[at, :], LANES - 1)
            high = jnp.right_shift(spot_idx[at, :], 7)
            found = [jnp.zeros((8, LANES), F32) if first else values[f, at, :] for f in range(FIELDS)]
            for code, fetch in rows:
                hit = high == code
                for f in range(FIELDS):
                    row = jnp.broadcast_to(fetch(f), (8, LANES))
                    found[f] = jnp.where(hit, lane_gather(row, low), found[f])
            for f in range(FIELDS):
                values[f, at, :] = found[f]

    look_up([(h, lambda f, h=h: state[f * 4 + h : f * 4 + h + 1, :]) for h in range(ROWS)], True)

    low_x, high_x = x > 0, x < count_x - 1
    low_y, high_y = y > 0, y < count_y - 1
    ghost_live = [low_x, high_x, low_y, high_y]
    back_live = [high_x, low_x, high_y, low_y]
    ghost_rows = []
    for k in range(SIDES):
        for r in range(2):
            code = jnp.where(ghost_live[k], 4 + 2 * k + r, -1) if k < 4 else 4 + 2 * (5 - layer) + r
            ghost_rows.append((code, lambda f, k=k, r=r: ghost_in[k, f : f + 1, r * LANES : (r + 1) * LANES]))
    for k in range(SIDES):
        halo_copy(k).wait_recv()
    look_up(ghost_rows, False)

    for r0 in (0, 8, 12):
        val = [[values[f, pl.ds(r0 * 4 + a, 8, stride=4), :] for a in range(4)] for f in range(FIELDS)]
        grad = [[grads[(3 * a + j) * 20 + r0 : (3 * a + j) * 20 + r0 + 8, :] for j in range(3)] for a in range(4)]
        vol = vol_rows[r0 : r0 + 8, :]
        vg = [[sum(val[i][a] * grad[a][j] for a in range(4)) for j in range(3)] for i in range(3)]
        strain = [[0.5 * (vg[i][j] + vg[j][i]) for j in range(3)] for i in range(3)]
        second = 0.5 * sum(strain[i][j] * strain[i][j] for i in range(3) for j in range(3))
        pm, tm, dm = [0.25 * (val[f][0] + val[f][1] + val[f][2] + val[f][3]) for f in (3, 4, 5)]
        visc2 = (1.0 - dm) * jnp.exp(-tm) * jnp.exp(jnp.log(second + strain_reg) * (-1.0 / 3.0))
        stress = [[visc2 * strain[i][j] - (pm if i == j else 0.0) for j in range(3)] for i in range(3)]
        cont = 0.25 * vol * (vg[0][0] + vg[1][1] + vg[2][2])
        for a in range(4):
            for c in range(4):
                if c < 3:
                    part = vol * sum(stress[c][j] * grad[a][j] for j in range(3))
                    if c == 2:
                        part = part + 0.25 * gravity * vol
                else:
                    part = cont
                for d in range(2):
                    contrib[pl.ds((r0 * 4 + a) * 8 + d * 4 + c, 8, stride=32), :] = part

    acc = jnp.zeros((128, LANES), F32)
    for t in range(SPOTS // 8):
        at = slice(t * 1024, (t + 1) * 1024)
        for u in range(8):
            s = t * 8 + u
            high = jnp.right_shift(jnp.broadcast_to(spot_idx[s : s + 1, :], (8, LANES)), 7) - half
            parts = split_two(contrib[s * 8 : (s + 1) * 8, :])
            hits = [high == 2 * m for m in range(8)]
            rows = [jnp.where(hits[m], parts[part], 0.0) for part in range(2) for m in range(8)]
            left[:, s * LANES : (s + 1) * LANES] = jnp.concatenate(rows, axis=0).astype(BF16)
        acc = acc + lax.dot_general(
            left[:, at], one_hot[:, at], (((1,), (1,)), ((), ())), preferred_element_type=F32
        )
    sums[...] = acc[0:64] + acc[64:128]

    def ret_copy(k):
        return pltpu.make_async_remote_copy(
            src_ref=ret_out.at[k],
            dst_ref=ret_in.at[k],
            send_sem=ret_send.at[k],
            recv_sem=ret_recv.at[k],
            device_id=backs[k],
            device_id_type=MESH,
        )

    for k in range(SIDES):
        ret_out[k] = sums[16 + 8 * k : 24 + 8 * k, :] if k < 4 else jnp.where(layer == 0, sums[56:64, :], sums[48:56, :])
        ret_copy(k).start()

    for k in range(SIDES):
        ret_copy(k).wait_recv()
        for r in range(2):
            u = k * 2 + r
            high = jnp.right_shift(jnp.broadcast_to(halo_idx[u : u + 1, :], (8, LANES)), 7) - half
            if k < 4:
                high = jnp.where(back_live[k], high, -2)
            four = ret_in[k, r * 4 : (r + 1) * 4, :]
            parts = split_two(jnp.concatenate([four, four], axis=0))
            rows = [jnp.where(high == 2 * m, part, 0.0) for part in parts for m in range(2)]
            left_back[:, u * LANES : (u + 1) * LANES] = jnp.concatenate(rows, axis=0).astype(BF16)
    back = lax.dot_general(left_back[...], halo_hot[...], (((1,), (1,)), ((), ())), preferred_element_type=F32)
    out[24:40, :] = sums[0:16, :] + back[0:16] + back[16:32]

    for peer in peers:
        block_copy(*peer).wait_send()
    for k in range(SIDES):
        halo_copy(k).wait_send()
        ret_copy(k).wait_send()


def per_device(old_state, send_blocks, node_slots, node_weights, front_mask, halo_lists, elem_nodes, shape_grads, elem_volume):
    count_x = lax.axis_size("mapx")
    count_y = lax.axis_size("mapy")
    vmem = pl.BlockSpec(memory_space=pltpu.VMEM)
    anywhere = pl.BlockSpec(memory_space=pl.ANY)
    dma = pltpu.SemaphoreType.DMA
    both = pl.pallas_call(
        functools.partial(kernel, count_x, count_y),
        out_shape=jax.ShapeDtypeStruct((40, LANES), F32),
        in_specs=[anywhere] * 9,
        out_specs=vmem,
        scratch_shapes=[
            pltpu.SMEM((10, 1, CAP), jnp.int32),
            pltpu.VMEM((FIELDS * 64, LANES), F32),
            pltpu.VMEM((4, 512), jnp.int32),
            pltpu.VMEM((4, 512), F32),
            pltpu.VMEM((ROWS, LANES), jnp.int32),
            pltpu.VMEM((6, 2, LANES), jnp.int32),
            pltpu.VMEM((4, 2560), jnp.int32),
            pltpu.VMEM((240, LANES), F32),
            pltpu.VMEM((5, 4, LANES), F32),
            pltpu.VMEM((10, CAP * FIELDS, LANES), F32),
            pltpu.VMEM((10, CAP * FIELDS, LANES), F32),
            pltpu.VMEM((16, LANES), jnp.int32),
            pltpu.VMEM((16, LANES), F32),
            pltpu.VMEM((32, LANES), F32),
            pltpu.VMEM((16, LANES), jnp.int32),
            pltpu.VMEM((SIDES, 8, WIDE), F32),
            pltpu.VMEM((SIDES, 8, WIDE), F32),
            pltpu.VMEM((SPOTS, LANES), jnp.int32),
            pltpu.VMEM((LANES, SPOTS * LANES), BF16),
            pltpu.VMEM((LANES, SIDES * WIDE), BF16),
            pltpu.VMEM((FIELDS, SPOTS, LANES), F32),
            pltpu.VMEM((24, LANES), F32),
            pltpu.VMEM((SPOTS * 8, LANES), F32),
            pltpu.VMEM((LANES, SPOTS * LANES), BF16),
            pltpu.VMEM((32, SIDES * WIDE), BF16),
            pltpu.VMEM((64, LANES), F32),
            pltpu.VMEM((SIDES, 8, LANES), F32),
            pltpu.VMEM((SIDES, 8, LANES), F32),
            dma((9,)),
            dma((10,)),
            dma((10,)),
            dma((SIDES,)),
            dma((SIDES,)),
            dma((SIDES,)),
            dma((SIDES,)),
        ],
        compiler_params=pltpu.CompilerParams(collective_id=0, has_side_effects=True),
        name="remap_residual",
    )(
        send_blocks.reshape(10, 1, CAP),
        old_state.reshape(FIELDS * 64, LANES),
        node_slots.reshape(4, 512),
        node_weights.reshape(4, 512),
        front_mask.reshape(ROWS, LANES),
        halo_lists.reshape(6, 2, LANES),
        elem_nodes.reshape(4, 2560),
        shape_grads.reshape(240, LANES),
        elem_volume.reshape(5, 4, LANES),
    )
    new_state = both[0:24].reshape(1, 1, 1, FIELDS, 512)
    residual = both[24:40].reshape(ROWS, 4, LANES).transpose(1, 0, 2).reshape(1, 1, 1, 4, 512)
    return new_state, residual


def solution(mesh):
    deep = P("mapx", "mapy", "layer", None, None)
    flat = P("mapx", "mapy", "layer", None)
    return jax.shard_map(
        per_device,
        mesh=mesh,
        in_specs=(deep, deep, deep, deep, flat, deep, deep, deep, flat),
        out_specs=(deep, deep),
        check_vma=False,
    )
```

```python
import functools

import jax
import jax.numpy as jnp
from jax import lax
from jax.experimental import pallas as pl
from jax.experimental.pallas import tpu as pltpu
from jax.sharding import PartitionSpec as P

MESH = pl.DeviceIdType.MESH
F32 = jnp.float32
BF16 = jnp.bfloat16
LANES = 128
WIDE = 256
FIELDS = 6
ROWS = 4
SIDES = 5
SPOTS = 80
CAP = 16

ocean_temp = 0.0
strain_reg = 0.01
gravity = 0.5


def lane_gather(row, lanes):
    return jnp.take_along_axis(row, lanes, axis=1)


def split_two(value):
    high = value.astype(BF16).astype(F32)
    return high, value - high


def lane_tile(s):
    return pl.ds(pl.multiple_of(s * LANES, LANES), LANES)


def kernel(
    count_x,
    count_y,
    blocks_in,
    old_in,
    slots_in,
    weights_in,
    front_in,
    halos_in,
    nodes_in,
    grads_in,
    volume_in,
    out,
    blocks,
    old,
    slots,
    weights,
    front,
    halos,
    nodes,
    grads,
    volume,
    block_out,
    block_in,
    lookup,
    weight_rows,
    state,
    halo_idx,
    halo_out,
    ghost_in,
    spot_idx,
    one_hot,
    halo_hot,
    values,
    vol_rows,
    contrib,
    left,
    left_back,
    sums,
    ret_out,
    ret_in,
    in_sem,
    block_send,
    block_recv,
    halo_send,
    halo_recv,
    ret_send,
    ret_recv,
):
    x = lax.axis_index("mapx")
    y = lax.axis_index("mapy")
    layer = lax.axis_index("layer")

    def device(dx, dy, which):
        return (lax.rem(x + dx + count_x, count_x), lax.rem(y + dy + count_y, count_y), which)

    far = [(t, lp) for t in (-2, 2, -1, 1) for lp in (0, 1)]
    peers = [((t + 2) * 2 + lp, (2 - t) * 2 + layer, device(t, 0, lp)) for t, lp in far]
    peers.append((4 + (1 - layer), 4 + layer, device(0, 0, 1 - layer)))
    sides = [device(1, 0, layer), device(-1, 0, layer), device(0, 1, layer), device(0, -1, layer), device(0, 0, 1 - layer)]
    backs = [sides[1], sides[0], sides[3], sides[2], sides[4]]

    barrier = pltpu.get_barrier_semaphore()
    greet = [peer[2] for peer in peers] + [sides[2], sides[3]]
    for other in greet:
        pl.semaphore_signal(barrier, inc=1, device_id=other, device_id_type=MESH)

    pairs_in = [
        (blocks_in, blocks),
        (old_in, old),
        (nodes_in, nodes),
        (halos_in, halos),
        (slots_in, slots),
        (weights_in, weights),
        (front_in, front),
        (grads_in, grads),
        (volume_in, volume),
    ]
    arrivals = [pltpu.make_async_copy(src, dst, in_sem.at[i]) for i, (src, dst) in enumerate(pairs_in)]
    for copy in arrivals:
        copy.start()

    arrivals[0].wait()
    arrivals[1].wait()
    pl.semaphore_wait(barrier, len(greet))

    def block_copy(number, theirs, other):
        return pltpu.make_async_remote_copy(
            src_ref=block_out.at[number],
            dst_ref=block_in.at[theirs],
            send_sem=block_send.at[number],
            recv_sem=block_recv.at[theirs],
            device_id=other,
            device_id_type=MESH,
        )

    def pack(number):
        for c in range(CAP):
            rows = old[pl.ds(blocks[number, 0, c], FIELDS, stride=64), :]
            block_out[number, c * FIELDS : (c + 1) * FIELDS, :] = rows

    for peer in peers:
        pack(peer[0])
        block_copy(*peer).start()
    me = 4 + layer
    pack(me)

    arrivals[2].wait()
    arrivals[3].wait()
    for j in range(20):
        spot_idx[pl.ds(j, 4, stride=20), :] = nodes[:, j * LANES : (j + 1) * LANES]
    for k in range(SIDES):
        halo_idx[k * 2 : k * 2 + 2, :] = halos[k] if k < 4 else halos[4 + layer]

    sub = lax.broadcasted_iota(jnp.int32, (8, LANES), 0)
    half = jnp.right_shift(sub, 2)

    def hot_tile(row):
        low = jnp.bitwise_and(jnp.broadcast_to(row, (8, LANES)), LANES - 1)
        return jnp.concatenate([jnp.where(low == sub + g * 8, 1.0, 0.0) for g in range(16)], axis=0).astype(BF16)

    def build_hot(s, carry):
        one_hot[:, lane_tile(s)] = hot_tile(spot_idx[pl.ds(s, 1), :])
        return carry

    def build_halo_hot(s, carry):
        halo_hot[:, lane_tile(s)] = hot_tile(halo_idx[pl.ds(s, 1), :])
        return carry

    lax.fori_loop(0, SPOTS, build_hot, 0, unroll=8)
    lax.fori_loop(0, SIDES * 2, build_halo_hot, 0, unroll=10)

    arrivals[4].wait()
    arrivals[5].wait()
    for j in range(ROWS):
        lookup[pl.ds(j, 4, stride=4), :] = slots[:, j * LANES : (j + 1) * LANES]
        weight_rows[pl.ds(j, 4, stride=4), :] = weights[:, j * LANES : (j + 1) * LANES]

    for copy in arrivals[6:]:
        copy.wait()
    for j in range(5):
        vol_rows[j * 4 : (j + 1) * 4, :] = volume[j]

    lo = [jnp.bitwise_and(lookup[v * 8 : (v + 1) * 8, :], LANES - 1) for v in range(2)]
    blk = [jnp.right_shift(lookup[v * 8 : (v + 1) * 8, :], 7) for v in range(2)]

    def interpolate(source, spot, number, acc):
        acc = list(acc)
        for c in range(CAP):
            hit = [blk[v] == number * CAP + c for v in range(2)]
            for f in range(FIELDS):
                row = jnp.broadcast_to(source[spot, c * FIELDS + f : c * FIELDS + f + 1, :], (8, LANES))
                for v in range(2):
                    acc[f * 2 + v] = jnp.where(hit[v], lane_gather(row, lo[v]), acc[f * 2 + v])
        return acc

    acc = tuple(jnp.zeros((8, LANES), F32) for _ in range(12))
    acc = interpolate(block_out, me, me, acc)
    for number, _, other in [peers[i] for i in (8, 0, 1, 2, 3, 4, 5, 6, 7)]:
        pltpu.make_async_remote_copy(
            src_ref=block_out.at[number],
            dst_ref=block_in.at[number],
            send_sem=block_send.at[number],
            recv_sem=block_recv.at[number],
            device_id=other,
            device_id_type=MESH,
        ).wait_recv()
        acc = interpolate(block_in, number, number, acc)

    for f in range(FIELDS):
        both = acc[f * 2] * weight_rows[0:8, :] + acc[f * 2 + 1] * weight_rows[8:16, :]
        total = both[0:4] + both[4:8]
        if f == 4:
            total = jnp.where(front[...] == 1, ocean_temp, total)
        state[f * 4 : (f + 1) * 4, :] = total
    state[24:32, :] = jnp.zeros((8, LANES), F32)
    tiles = [state[pl.ds(h, 8, stride=4), :] for h in range(ROWS)]

    def halo_copy(k):
        return pltpu.make_async_remote_copy(
            src_ref=halo_out.at[k],
            dst_ref=ghost_in.at[k],
            send_sem=halo_send.at[k],
            recv_sem=halo_recv.at[k],
            device_id=sides[k],
            device_id_type=MESH,
        )

    for k in range(SIDES):
        for r in range(2):
            idx = jnp.broadcast_to(halo_idx[k * 2 + r : k * 2 + r + 1, :], (8, LANES))
            low = jnp.bitwise_and(idx, LANES - 1)
            high = jnp.right_shift(idx, 7)
            kept = jnp.zeros((8, LANES), F32)
            for h in range(ROWS):
                kept = jnp.where(high == h, lane_gather(tiles[h], low), kept)
            halo_out[k, :, r * LANES : (r + 1) * LANES] = kept
        halo_copy(k).start()

    out[0:24, :] = state[0:24, :]

    def look_up(rows, first):
        for t in range(SPOTS // 8):
            at = slice(t * 8, (t + 1) * 8)
            low = jnp.bitwise_and(spot_idx[at, :], LANES - 1)
            high = jnp.right_shift(spot_idx[at, :], 7)
            found = [jnp.zeros((8, LANES), F32) if first else values[f, at, :] for f in range(FIELDS)]
            for code, fetch in rows:
                hit = high == code
                for f in range(FIELDS):
                    row = jnp.broadcast_to(fetch(f), (8, LANES))
                    found[f] = jnp.where(hit, lane_gather(row, low), found[f])
            for f in range(FIELDS):
                values[f, at, :] = found[f]

    look_up([(h, lambda f, h=h: state[f * 4 + h : f * 4 + h + 1, :]) for h in range(ROWS)], True)

    low_x, high_x = x > 0, x < count_x - 1
    low_y, high_y = y > 0, y < count_y - 1
    ghost_live = [low_x, high_x, low_y, high_y]
    back_live = [high_x, low_x, high_y, low_y]
    ghost_rows = []
    for k in range(SIDES):
        for r in range(2):
            code = jnp.where(ghost_live[k], 4 + 2 * k + r, -1) if k < 4 else 4 + 2 * (5 - layer) + r
            ghost_rows.append((code, lambda f, k=k, r=r: ghost_in[k, f : f + 1, r * LANES : (r + 1) * LANES]))
    for k in range(SIDES):
        halo_copy(k).wait_recv()
    look_up(ghost_rows, False)

    def add_sums(acc, first, last):
        for s in range(first, last):
            high = jnp.right_shift(jnp.broadcast_to(spot_idx[s : s + 1, :], (8, LANES)), 7)
            hits = [high == sub + 8 * m for m in range(2)]
            parts = [split_two(jnp.broadcast_to(contrib[c, s : s + 1, :], (8, LANES))) for c in range(4)]
            rows = [jnp.where(hits[m], parts[c][p], 0.0) for p in range(2) for c in range(4) for m in range(2)]
            left[:, s * LANES : (s + 1) * LANES] = jnp.concatenate(rows, axis=0).astype(BF16)
        at = slice(first * LANES, last * LANES)
        return acc + lax.dot_general(
            left[:, at], one_hot[:, at], (((1,), (1,)), ((), ())), preferred_element_type=F32
        )

    acc = jnp.zeros((LANES, LANES), F32)
    for r0, r1 in ((0, 0), (8, 8), (12, 16)):
        val = [[values[f, a * 20 + r0 : a * 20 + r0 + 8, :] for a in range(4)] for f in range(FIELDS)]
        grad = [[grads[(3 * a + j) * 20 + r0 : (3 * a + j) * 20 + r0 + 8, :] for j in range(3)] for a in range(4)]
        vol = vol_rows[r0 : r0 + 8, :]
        vg = [[sum(val[i][a] * grad[a][j] for a in range(4)) for j in range(3)] for i in range(3)]
        strain = [[0.5 * (vg[i][j] + vg[j][i]) for j in range(3)] for i in range(3)]
        second = 0.5 * sum(strain[i][j] * strain[i][j] for i in range(3) for j in range(3))
        pm, tm, dm = [0.25 * (val[f][0] + val[f][1] + val[f][2] + val[f][3]) for f in (3, 4, 5)]
        visc2 = (1.0 - dm) * jnp.exp(-tm) * jnp.exp(jnp.log(second + strain_reg) * (-1.0 / 3.0))
        stress = [[visc2 * strain[i][j] - (pm if i == j else 0.0) for j in range(3)] for i in range(3)]
        cont = 0.25 * vol * (vg[0][0] + vg[1][1] + vg[2][2])
        for a in range(4):
            for c in range(4):
                if c < 3:
                    part = vol * sum(stress[c][j] * grad[a][j] for j in range(3))
                    if c == 2:
                        part = part + 0.25 * gravity * vol
                else:
                    part = cont
                contrib[c, a * 20 + r0 : a * 20 + r0 + 8, :] = part
        for a in range(4):
            acc = add_sums(acc, a * 20 + r1, a * 20 + r0 + 8)

    sums[...] = acc[0:64] + acc[64:128]

    def ret_copy(k):
        return pltpu.make_async_remote_copy(
            src_ref=ret_out.at[k],
            dst_ref=ret_in.at[k],
            send_sem=ret_send.at[k],
            recv_sem=ret_recv.at[k],
            device_id=backs[k],
            device_id_type=MESH,
        )

    for k in range(SIDES):
        for r in range(2):
            row = 4 + 2 * k + r
            part = sums[pl.ds(row, 4, stride=16), :]
            if k == 4:
                part = jnp.where(layer == 0, sums[pl.ds(row + 2, 4, stride=16), :], part)
            ret_out[k, r * 4 : (r + 1) * 4, :] = part
        ret_copy(k).start()

    for k in range(SIDES):
        ret_copy(k).wait_recv()
        for r in range(2):
            u = k * 2 + r
            high = jnp.right_shift(jnp.broadcast_to(halo_idx[u : u + 1, :], (8, LANES)), 7) - half
            if k < 4:
                high = jnp.where(back_live[k], high, -2)
            four = ret_in[k, r * 4 : (r + 1) * 4, :]
            parts = split_two(jnp.concatenate([four, four], axis=0))
            rows = [jnp.where(high == 2 * m, part, 0.0) for part in parts for m in range(2)]
            left_back[:, u * LANES : (u + 1) * LANES] = jnp.concatenate(rows, axis=0).astype(BF16)
    back = lax.dot_general(left_back[...], halo_hot[...], (((1,), (1,)), ((), ())), preferred_element_type=F32)
    back = back[0:16] + back[16:32]
    for h in range(ROWS):
        out[24 + h * 4 : 28 + h * 4, :] = sums[pl.ds(h, 4, stride=16), :] + back[h * 4 : (h + 1) * 4]

    for peer in peers:
        block_copy(*peer).wait_send()
    for k in range(SIDES):
        halo_copy(k).wait_send()
        ret_copy(k).wait_send()


def write_outputs(both, out_new, out_res):
    out_new[...] = both[0:24, :]
    out_res[...] = both[24:40, :]


def per_device(old_state, send_blocks, node_slots, node_weights, front_mask, halo_lists, elem_nodes, shape_grads, elem_volume):
    count_x = lax.axis_size("mapx")
    count_y = lax.axis_size("mapy")
    vmem = pl.BlockSpec(memory_space=pltpu.VMEM)
    anywhere = pl.BlockSpec(memory_space=pl.ANY)
    dma = pltpu.SemaphoreType.DMA
    both = pl.pallas_call(
        functools.partial(kernel, count_x, count_y),
        out_shape=jax.ShapeDtypeStruct((40, LANES), F32),
        in_specs=[anywhere] * 9,
        out_specs=vmem,
        scratch_shapes=[
            pltpu.SMEM((10, 1, CAP), jnp.int32),
            pltpu.VMEM((FIELDS * 64, LANES), F32),
            pltpu.VMEM((4, 512), jnp.int32),
            pltpu.VMEM((4, 512), F32),
            pltpu.VMEM((ROWS, LANES), jnp.int32),
            pltpu.VMEM((6, 2, LANES), jnp.int32),
            pltpu.VMEM((4, 2560), jnp.int32),
            pltpu.VMEM((240, LANES), F32),
            pltpu.VMEM((5, 4, LANES), F32),
            pltpu.VMEM((10, CAP * FIELDS, LANES), F32),
            pltpu.VMEM((10, CAP * FIELDS, LANES), F32),
            pltpu.VMEM((16, LANES), jnp.int32),
            pltpu.VMEM((16, LANES), F32),
            pltpu.VMEM((32, LANES), F32),
            pltpu.VMEM((16, LANES), jnp.int32),
            pltpu.VMEM((SIDES, 8, WIDE), F32),
            pltpu.VMEM((SIDES, 8, WIDE), F32),
            pltpu.VMEM((SPOTS, LANES), jnp.int32),
            pltpu.VMEM((LANES, SPOTS * LANES), BF16),
            pltpu.VMEM((LANES, SIDES * WIDE), BF16),
            pltpu.VMEM((FIELDS, SPOTS, LANES), F32),
            pltpu.VMEM((24, LANES), F32),
            pltpu.VMEM((4, SPOTS, LANES), F32),
            pltpu.VMEM((LANES, SPOTS * LANES), BF16),
            pltpu.VMEM((32, SIDES * WIDE), BF16),
            pltpu.VMEM((64, LANES), F32),
            pltpu.VMEM((SIDES, 8, LANES), F32),
            pltpu.VMEM((SIDES, 8, LANES), F32),
            dma((9,)),
            dma((10,)),
            dma((10,)),
            dma((SIDES,)),
            dma((SIDES,)),
            dma((SIDES,)),
            dma((SIDES,)),
        ],
        compiler_params=pltpu.CompilerParams(collective_id=0, has_side_effects=True),
        name="remap_residual",
    )(
        send_blocks.reshape(10, 1, CAP),
        old_state.reshape(FIELDS * 64, LANES),
        node_slots.reshape(4, 512),
        node_weights.reshape(4, 512),
        front_mask.reshape(ROWS, LANES),
        halo_lists.reshape(6, 2, LANES),
        elem_nodes.reshape(4, 2560),
        shape_grads.reshape(240, LANES),
        elem_volume.reshape(5, 4, LANES),
    )
    new_state, residual = pl.pallas_call(
        write_outputs,
        out_shape=(jax.ShapeDtypeStruct((24, LANES), F32), jax.ShapeDtypeStruct((16, LANES), F32)),
        in_specs=[vmem],
        out_specs=(vmem, vmem),
        name="write_outputs",
    )(both)
    residual = residual.reshape(ROWS, 4, LANES).transpose(1, 0, 2)
    return new_state.reshape(1, 1, 1, FIELDS, 512), residual.reshape(1, 1, 1, 4, 512)


def solution(mesh):
    deep = P("mapx", "mapy", "layer", None, None)
    flat = P("mapx", "mapy", "layer", None)
    return jax.shard_map(
        per_device,
        mesh=mesh,
        in_specs=(deep, deep, deep, deep, flat, deep, deep, deep, flat),
        out_specs=(deep, deep),
        check_vma=False,
    )
```

```python
import functools

import jax
import jax.numpy as jnp
from jax import lax
from jax.experimental import pallas as pl
from jax.experimental.pallas import tpu as pltpu
from jax.sharding import PartitionSpec as P

MESH = pl.DeviceIdType.MESH
F32 = jnp.float32
BF16 = jnp.bfloat16
LANES = 128
WIDE = 256
FIELDS = 6
ROWS = 4
SIDES = 5
SPOTS = 80
CAP = 16

ocean_temp = 0.0
strain_reg = 0.01
gravity = 0.5


def lane_gather(row, lanes):
    return jnp.take_along_axis(row, lanes, axis=1)


def split_two(value):
    high = value.astype(BF16).astype(F32)
    return high, value - high


def lane_tile(s):
    return pl.ds(pl.multiple_of(s * LANES, LANES), LANES)


def kernel(
    count_x,
    count_y,
    blocks_in,
    old_in,
    slots_in,
    weights_in,
    front_in,
    halos_in,
    nodes_in,
    grads_in,
    volume_in,
    out_any,
    blocks,
    old,
    slots,
    weights,
    front,
    halos,
    nodes,
    grads,
    volume,
    block_out,
    block_in,
    lookup,
    weight_rows,
    state,
    halo_idx,
    halo_out,
    ghost_in,
    spot_idx,
    one_hot,
    halo_hot,
    values,
    vol_rows,
    contrib,
    left,
    left_back,
    sums,
    ret_out,
    ret_in,
    out,
    in_sem,
    block_send,
    block_recv,
    halo_send,
    halo_recv,
    ret_send,
    ret_recv,
):
    x = lax.axis_index("mapx")
    y = lax.axis_index("mapy")
    layer = lax.axis_index("layer")

    def device(dx, dy, which):
        return (lax.rem(x + dx + count_x, count_x), lax.rem(y + dy + count_y, count_y), which)

    far = [(t, lp) for t in (-2, 2, -1, 1) for lp in (0, 1)]
    peers = [((t + 2) * 2 + lp, (2 - t) * 2 + layer, device(t, 0, lp)) for t, lp in far]
    peers.append((4 + (1 - layer), 4 + layer, device(0, 0, 1 - layer)))
    sides = [device(1, 0, layer), device(-1, 0, layer), device(0, 1, layer), device(0, -1, layer), device(0, 0, 1 - layer)]
    backs = [sides[1], sides[0], sides[3], sides[2], sides[4]]

    barrier = pltpu.get_barrier_semaphore()
    greet = [peer[2] for peer in peers] + [sides[2], sides[3]]
    for other in greet:
        pl.semaphore_signal(barrier, inc=1, device_id=other, device_id_type=MESH)

    pairs_in = [
        (blocks_in, blocks),
        (old_in, old),
        (nodes_in, nodes),
        (halos_in, halos),
        (slots_in, slots),
        (weights_in, weights),
        (front_in, front),
        (grads_in, grads),
        (volume_in, volume),
    ]
    arrivals = [pltpu.make_async_copy(src, dst, in_sem.at[i]) for i, (src, dst) in enumerate(pairs_in)]
    for copy in arrivals:
        copy.start()

    arrivals[0].wait()
    arrivals[1].wait()
    pl.semaphore_wait(barrier, len(greet))

    def block_copy(number, theirs, other):
        return pltpu.make_async_remote_copy(
            src_ref=block_out.at[number],
            dst_ref=block_in.at[theirs],
            send_sem=block_send.at[number],
            recv_sem=block_recv.at[theirs],
            device_id=other,
            device_id_type=MESH,
        )

    def pack(number):
        for c in range(CAP):
            rows = old[pl.ds(blocks[number, 0, c], FIELDS, stride=64), :]
            block_out[number, c * FIELDS : (c + 1) * FIELDS, :] = rows

    for peer in peers:
        pack(peer[0])
        block_copy(*peer).start()
    me = 4 + layer
    pack(me)

    arrivals[2].wait()
    arrivals[3].wait()
    for j in range(20):
        spot_idx[pl.ds(j, 4, stride=20), :] = nodes[:, j * LANES : (j + 1) * LANES]
    for k in range(SIDES):
        halo_idx[k * 2 : k * 2 + 2, :] = halos[k] if k < 4 else halos[4 + layer]

    sub = lax.broadcasted_iota(jnp.int32, (8, LANES), 0)
    half = jnp.right_shift(sub, 2)

    def hot_tile(row):
        low = jnp.bitwise_and(jnp.broadcast_to(row, (8, LANES)), LANES - 1)
        return jnp.concatenate([jnp.where(low == sub + g * 8, 1.0, 0.0) for g in range(16)], axis=0).astype(BF16)

    def build_hot(s, carry):
        one_hot[:, lane_tile(s)] = hot_tile(spot_idx[pl.ds(s, 1), :])
        return carry

    def build_halo_hot(s, carry):
        halo_hot[:, lane_tile(s)] = hot_tile(halo_idx[pl.ds(s, 1), :])
        return carry

    lax.fori_loop(0, SPOTS, build_hot, 0, unroll=8)
    lax.fori_loop(0, SIDES * 2, build_halo_hot, 0, unroll=10)

    arrivals[4].wait()
    arrivals[5].wait()
    for j in range(ROWS):
        lookup[pl.ds(j, 4, stride=4), :] = slots[:, j * LANES : (j + 1) * LANES]
        weight_rows[pl.ds(j, 4, stride=4), :] = weights[:, j * LANES : (j + 1) * LANES]

    for copy in arrivals[6:]:
        copy.wait()
    for j in range(5):
        vol_rows[j * 4 : (j + 1) * 4, :] = volume[j]

    lo = [jnp.bitwise_and(lookup[v * 8 : (v + 1) * 8, :], LANES - 1) for v in range(2)]
    blk = [jnp.right_shift(lookup[v * 8 : (v + 1) * 8, :], 7) for v in range(2)]

    def interpolate(source, spot, number, acc):
        acc = list(acc)
        for c in range(CAP):
            hit = [blk[v] == number * CAP + c for v in range(2)]
            for f in range(FIELDS):
                row = jnp.broadcast_to(source[spot, c * FIELDS + f : c * FIELDS + f + 1, :], (8, LANES))
                for v in range(2):
                    acc[f * 2 + v] = jnp.where(hit[v], lane_gather(row, lo[v]), acc[f * 2 + v])
        return acc

    acc = tuple(jnp.zeros((8, LANES), F32) for _ in range(12))
    acc = interpolate(block_out, me, me, acc)
    for number, _, other in [peers[i] for i in (8, 0, 1, 2, 3, 4, 5, 6, 7)]:
        pltpu.make_async_remote_copy(
            src_ref=block_out.at[number],
            dst_ref=block_in.at[number],
            send_sem=block_send.at[number],
            recv_sem=block_recv.at[number],
            device_id=other,
            device_id_type=MESH,
        ).wait_recv()
        acc = interpolate(block_in, number, number, acc)

    for f in range(FIELDS):
        both = acc[f * 2] * weight_rows[0:8, :] + acc[f * 2 + 1] * weight_rows[8:16, :]
        total = both[0:4] + both[4:8]
        if f == 4:
            total = jnp.where(front[...] == 1, ocean_temp, total)
        state[f * 4 : (f + 1) * 4, :] = total
    state[24:32, :] = jnp.zeros((8, LANES), F32)
    tiles = [state[pl.ds(h, 8, stride=4), :] for h in range(ROWS)]

    def halo_copy(k):
        return pltpu.make_async_remote_copy(
            src_ref=halo_out.at[k],
            dst_ref=ghost_in.at[k],
            send_sem=halo_send.at[k],
            recv_sem=halo_recv.at[k],
            device_id=sides[k],
            device_id_type=MESH,
        )

    for k in range(SIDES):
        for r in range(2):
            idx = jnp.broadcast_to(halo_idx[k * 2 + r : k * 2 + r + 1, :], (8, LANES))
            low = jnp.bitwise_and(idx, LANES - 1)
            high = jnp.right_shift(idx, 7)
            kept = jnp.zeros((8, LANES), F32)
            for h in range(ROWS):
                kept = jnp.where(high == h, lane_gather(tiles[h], low), kept)
            halo_out[k, :, r * LANES : (r + 1) * LANES] = kept
        halo_copy(k).start()

    out[0:24, :] = state[0:24, :]
    early = pltpu.make_async_copy(out.at[0:24], out_any.at[0:24], in_sem.at[9])
    early.start()

    def look_up(rows, first):
        for t in range(SPOTS // 8):
            at = slice(t * 8, (t + 1) * 8)
            low = jnp.bitwise_and(spot_idx[at, :], LANES - 1)
            high = jnp.right_shift(spot_idx[at, :], 7)
            found = [jnp.zeros((8, LANES), F32) if first else values[f, at, :] for f in range(FIELDS)]
            for code, fetch in rows:
                hit = high == code
                for f in range(FIELDS):
                    row = jnp.broadcast_to(fetch(f), (8, LANES))
                    found[f] = jnp.where(hit, lane_gather(row, low), found[f])
            for f in range(FIELDS):
                values[f, at, :] = found[f]

    look_up([(h, lambda f, h=h: state[f * 4 + h : f * 4 + h + 1, :]) for h in range(ROWS)], True)

    low_x, high_x = x > 0, x < count_x - 1
    low_y, high_y = y > 0, y < count_y - 1
    ghost_live = [low_x, high_x, low_y, high_y]
    back_live = [high_x, low_x, high_y, low_y]
    for k in (4, 0, 1, 2, 3):
        ghost_rows = []
        for r in range(2):
            code = jnp.where(ghost_live[k], 4 + 2 * k + r, -1) if k < 4 else 4 + 2 * (5 - layer) + r
            ghost_rows.append((code, lambda f, k=k, r=r: ghost_in[k, f : f + 1, r * LANES : (r + 1) * LANES]))
        halo_copy(k).wait_recv()
        look_up(ghost_rows, False)

    def add_sums(acc, first, last):
        for s in range(first, last):
            high = jnp.right_shift(jnp.broadcast_to(spot_idx[s : s + 1, :], (8, LANES)), 7)
            hits = [high == sub + 8 * m for m in range(2)]
            parts = [split_two(jnp.broadcast_to(contrib[c, s : s + 1, :], (8, LANES))) for c in range(4)]
            rows = [jnp.where(hits[m], parts[c][p], 0.0) for p in range(2) for c in range(4) for m in range(2)]
            left[:, s * LANES : (s + 1) * LANES] = jnp.concatenate(rows, axis=0).astype(BF16)
        at = slice(first * LANES, last * LANES)
        return acc + lax.dot_general(
            left[:, at], one_hot[:, at], (((1,), (1,)), ((), ())), preferred_element_type=F32
        )

    acc = jnp.zeros((LANES, LANES), F32)
    for r0, r1 in ((0, 0), (8, 8), (12, 16)):
        val = [[values[f, a * 20 + r0 : a * 20 + r0 + 8, :] for a in range(4)] for f in range(FIELDS)]
        grad = [[grads[(3 * a + j) * 20 + r0 : (3 * a + j) * 20 + r0 + 8, :] for j in range(3)] for a in range(4)]
        vol = vol_rows[r0 : r0 + 8, :]
        vg = [[sum(val[i][a] * grad[a][j] for a in range(4)) for j in range(3)] for i in range(3)]
        strain = [[0.5 * (vg[i][j] + vg[j][i]) for j in range(3)] for i in range(3)]
        second = 0.5 * sum(strain[i][j] * strain[i][j] for i in range(3) for j in range(3))
        pm, tm, dm = [0.25 * (val[f][0] + val[f][1] + val[f][2] + val[f][3]) for f in (3, 4, 5)]
        visc2 = (1.0 - dm) * jnp.exp(-tm) * jnp.exp(jnp.log(second + strain_reg) * (-1.0 / 3.0))
        stress = [[visc2 * strain[i][j] - (pm if i == j else 0.0) for j in range(3)] for i in range(3)]
        cont = 0.25 * vol * (vg[0][0] + vg[1][1] + vg[2][2])
        for a in range(4):
            for c in range(4):
                if c < 3:
                    part = vol * sum(stress[c][j] * grad[a][j] for j in range(3))
                    if c == 2:
                        part = part + 0.25 * gravity * vol
                else:
                    part = cont
                contrib[c, a * 20 + r0 : a * 20 + r0 + 8, :] = part
        for a in range(4):
            acc = add_sums(acc, a * 20 + r1, a * 20 + r0 + 8)

    sums[...] = acc[0:64] + acc[64:128]

    def ret_copy(k):
        return pltpu.make_async_remote_copy(
            src_ref=ret_out.at[k],
            dst_ref=ret_in.at[k],
            send_sem=ret_send.at[k],
            recv_sem=ret_recv.at[k],
            device_id=backs[k],
            device_id_type=MESH,
        )

    for k in range(SIDES):
        for r in range(2):
            row = 4 + 2 * k + r
            part = sums[pl.ds(row, 4, stride=16), :]
            if k == 4:
                part = jnp.where(layer == 0, sums[pl.ds(row + 2, 4, stride=16), :], part)
            ret_out[k, r * 4 : (r + 1) * 4, :] = part
        ret_copy(k).start()

    for k in range(SIDES):
        ret_copy(k).wait_recv()
        for r in range(2):
            u = k * 2 + r
            high = jnp.right_shift(jnp.broadcast_to(halo_idx[u : u + 1, :], (8, LANES)), 7) - half
            if k < 4:
                high = jnp.where(back_live[k], high, -2)
            four = ret_in[k, r * 4 : (r + 1) * 4, :]
            parts = split_two(jnp.concatenate([four, four], axis=0))
            rows = [jnp.where(high == 2 * m, part, 0.0) for part in parts for m in range(2)]
            left_back[:, u * LANES : (u + 1) * LANES] = jnp.concatenate(rows, axis=0).astype(BF16)
    back = lax.dot_general(left_back[...], halo_hot[...], (((1,), (1,)), ((), ())), preferred_element_type=F32)
    back = back[0:16] + back[16:32]
    for h in range(ROWS):
        out[24 + h * 4 : 28 + h * 4, :] = sums[pl.ds(h, 4, stride=16), :] + back[h * 4 : (h + 1) * 4]

    late = pltpu.make_async_copy(out.at[24:40], out_any.at[24:40], in_sem.at[10])
    late.start()
    for peer in peers:
        block_copy(*peer).wait_send()
    for k in range(SIDES):
        halo_copy(k).wait_send()
        ret_copy(k).wait_send()
    early.wait()
    late.wait()


def write_outputs(both, out_new, out_res):
    out_new[...] = both[0:24, :]
    out_res[...] = both[24:40, :]


def per_device(old_state, send_blocks, node_slots, node_weights, front_mask, halo_lists, elem_nodes, shape_grads, elem_volume):
    count_x = lax.axis_size("mapx")
    count_y = lax.axis_size("mapy")
    vmem = pl.BlockSpec(memory_space=pltpu.VMEM)
    far_memory = pl.BlockSpec(memory_space=pltpu.HBM)
    dma = pltpu.SemaphoreType.DMA
    both = pl.pallas_call(
        functools.partial(kernel, count_x, count_y),
        out_shape=jax.ShapeDtypeStruct((40, LANES), F32),
        in_specs=[far_memory] * 9,
        out_specs=pl.BlockSpec(memory_space=pl.ANY),
        scratch_shapes=[
            pltpu.SMEM((10, 1, CAP), jnp.int32),
            pltpu.VMEM((FIELDS * 64, LANES), F32),
            pltpu.VMEM((4, 512), jnp.int32),
            pltpu.VMEM((4, 512), F32),
            pltpu.VMEM((ROWS, LANES), jnp.int32),
            pltpu.VMEM((6, 2, LANES), jnp.int32),
            pltpu.VMEM((4, 2560), jnp.int32),
            pltpu.VMEM((240, LANES), F32),
            pltpu.VMEM((5, 4, LANES), F32),
            pltpu.VMEM((10, CAP * FIELDS, LANES), F32),
            pltpu.VMEM((10, CAP * FIELDS, LANES), F32),
            pltpu.VMEM((16, LANES), jnp.int32),
            pltpu.VMEM((16, LANES), F32),
            pltpu.VMEM((32, LANES), F32),
            pltpu.VMEM((16, LANES), jnp.int32),
            pltpu.VMEM((SIDES, 8, WIDE), F32),
            pltpu.VMEM((SIDES, 8, WIDE), F32),
            pltpu.VMEM((SPOTS, LANES), jnp.int32),
            pltpu.VMEM((LANES, SPOTS * LANES), BF16),
            pltpu.VMEM((LANES, SIDES * WIDE), BF16),
            pltpu.VMEM((FIELDS, SPOTS, LANES), F32),
            pltpu.VMEM((24, LANES), F32),
            pltpu.VMEM((4, SPOTS, LANES), F32),
            pltpu.VMEM((LANES, SPOTS * LANES), BF16),
            pltpu.VMEM((32, SIDES * WIDE), BF16),
            pltpu.VMEM((64, LANES), F32),
            pltpu.VMEM((SIDES, 8, LANES), F32),
            pltpu.VMEM((SIDES, 8, LANES), F32),
            pltpu.VMEM((40, LANES), F32),
            dma((11,)),
            dma((10,)),
            dma((10,)),
            dma((SIDES,)),
            dma((SIDES,)),
            dma((SIDES,)),
            dma((SIDES,)),
        ],
        compiler_params=pltpu.CompilerParams(collective_id=0, has_side_effects=True, vmem_limit_bytes=24 << 20),
        name="remap_residual",
    )(
        *(
            pltpu.with_memory_space_constraint(value, pltpu.HBM)
            for value in (
                send_blocks.reshape(10, 1, CAP),
                old_state.reshape(FIELDS * 64, LANES),
                node_slots.reshape(4, 512),
                node_weights.reshape(4, 512),
                front_mask.reshape(ROWS, LANES),
                halo_lists.reshape(6, 2, LANES),
                elem_nodes.reshape(4, 2560),
                shape_grads.reshape(240, LANES),
                elem_volume.reshape(5, 4, LANES),
            )
        )
    )
    new_state, residual = pl.pallas_call(
        write_outputs,
        out_shape=(jax.ShapeDtypeStruct((24, LANES), F32), jax.ShapeDtypeStruct((16, LANES), F32)),
        in_specs=[vmem],
        out_specs=(vmem, vmem),
        compiler_params=pltpu.CompilerParams(vmem_limit_bytes=1 << 20),
        name="write_outputs",
    )(both)
    residual = residual.reshape(ROWS, 4, LANES).transpose(1, 0, 2)
    return new_state.reshape(1, 1, 1, FIELDS, 512), residual.reshape(1, 1, 1, 4, 512)


def solution(mesh):
    deep = P("mapx", "mapy", "layer", None, None)
    flat = P("mapx", "mapy", "layer", None)
    return jax.shard_map(
        per_device,
        mesh=mesh,
        in_specs=(deep, deep, deep, deep, flat, deep, deep, deep, flat),
        out_specs=(deep, deep),
        check_vma=False,
    )
```

```python
import functools

import jax
import jax.numpy as jnp
from jax import lax
from jax.experimental import pallas as pl
from jax.experimental.pallas import tpu as pltpu
from jax.sharding import PartitionSpec as P

MESH = pl.DeviceIdType.MESH
F32 = jnp.float32
BF16 = jnp.bfloat16
LANES = 128
WIDE = 256
FIELDS = 6
ROWS = 4
SIDES = 5
SPOTS = 80
CAP = 16

ocean_temp = 0.0
strain_reg = 0.01
gravity = 0.5


def lane_gather(row, lanes):
    return jnp.take_along_axis(row, lanes, axis=1)


def split_two(value):
    high = value.astype(BF16).astype(F32)
    return high, value - high


def lane_tile(s):
    return pl.ds(pl.multiple_of(s * LANES, LANES), LANES)


def kernel(
    count_x,
    count_y,
    blocks_in,
    old_in,
    slots_in,
    weights_in,
    front_in,
    halos_in,
    nodes_in,
    grads_in,
    volume_in,
    out,
    blocks,
    old,
    slots,
    weights,
    front,
    halos,
    nodes,
    grads,
    volume,
    block_out,
    block_in,
    lookup,
    weight_rows,
    state,
    halo_idx,
    halo_out,
    ghost_in,
    spot_idx,
    one_hot,
    halo_hot,
    values,
    vol_rows,
    contrib,
    left,
    left_back,
    sums,
    ret_out,
    ret_in,
    in_sem,
    block_send,
    block_recv,
    halo_send,
    halo_recv,
    ret_send,
    ret_recv,
):
    x = lax.axis_index("mapx")
    y = lax.axis_index("mapy")
    layer = lax.axis_index("layer")

    def device(dx, dy, which):
        return (lax.rem(x + dx + count_x, count_x), lax.rem(y + dy + count_y, count_y), which)

    far = [(t, lp) for t in (-2, 2, -1, 1) for lp in (0, 1)]
    peers = [((t + 2) * 2 + lp, (2 - t) * 2 + layer, device(t, 0, lp)) for t, lp in far]
    peers.append((4 + (1 - layer), 4 + layer, device(0, 0, 1 - layer)))
    sides = [device(1, 0, layer), device(-1, 0, layer), device(0, 1, layer), device(0, -1, layer), device(0, 0, 1 - layer)]
    backs = [sides[1], sides[0], sides[3], sides[2], sides[4]]

    barrier = pltpu.get_barrier_semaphore()
    greet = [peer[2] for peer in peers] + [sides[2], sides[3]]
    for other in greet:
        pl.semaphore_signal(barrier, inc=1, device_id=other, device_id_type=MESH)

    pairs_in = [
        (blocks_in, blocks),
        (old_in, old),
        (nodes_in, nodes),
        (halos_in, halos),
        (slots_in, slots),
        (weights_in, weights),
        (front_in, front),
        (grads_in, grads),
        (volume_in, volume),
    ]
    arrivals = [pltpu.make_async_copy(src, dst, in_sem.at[i]) for i, (src, dst) in enumerate(pairs_in)]
    for copy in arrivals:
        copy.start()

    arrivals[0].wait()
    arrivals[1].wait()
    def block_copy(number, theirs, other):
        return pltpu.make_async_remote_copy(
            src_ref=block_out.at[number],
            dst_ref=block_in.at[theirs],
            send_sem=block_send.at[number],
            recv_sem=block_recv.at[theirs],
            device_id=other,
            device_id_type=MESH,
        )

    def pack(number):
        for c in range(CAP):
            rows = old[pl.ds(blocks[number, 0, c], FIELDS, stride=64), :]
            block_out[number, c * FIELDS : (c + 1) * FIELDS, :] = rows

    for number in range(10):
        pack(number)
    me = 4 + layer
    pl.semaphore_wait(barrier, len(greet))
    for peer in peers:
        block_copy(*peer).start()

    arrivals[2].wait()
    arrivals[3].wait()
    for j in range(20):
        spot_idx[pl.ds(j, 4, stride=20), :] = nodes[:, j * LANES : (j + 1) * LANES]
    for k in range(SIDES):
        halo_idx[k * 2 : k * 2 + 2, :] = halos[k] if k < 4 else halos[4 + layer]

    sub = lax.broadcasted_iota(jnp.int32, (8, LANES), 0)
    half = jnp.right_shift(sub, 2)

    def hot_tile(row):
        low = jnp.bitwise_and(jnp.broadcast_to(row, (8, LANES)), LANES - 1)
        return jnp.concatenate([jnp.where(low == sub + g * 8, 1.0, 0.0) for g in range(16)], axis=0).astype(BF16)

    def build_hot(s, carry):
        one_hot[:, lane_tile(s)] = hot_tile(spot_idx[pl.ds(s, 1), :])
        return carry

    def build_halo_hot(s, carry):
        halo_hot[:, lane_tile(s)] = hot_tile(halo_idx[pl.ds(s, 1), :])
        return carry

    lax.fori_loop(0, SPOTS, build_hot, 0, unroll=8)
    lax.fori_loop(0, SIDES * 2, build_halo_hot, 0, unroll=10)

    arrivals[4].wait()
    arrivals[5].wait()
    for j in range(ROWS):
        lookup[pl.ds(j, 4, stride=4), :] = slots[:, j * LANES : (j + 1) * LANES]
        weight_rows[pl.ds(j, 4, stride=4), :] = weights[:, j * LANES : (j + 1) * LANES]

    for copy in arrivals[6:]:
        copy.wait()
    for j in range(5):
        vol_rows[j * 4 : (j + 1) * 4, :] = volume[j]

    lo = [jnp.bitwise_and(lookup[v * 8 : (v + 1) * 8, :], LANES - 1) for v in range(2)]
    blk = [jnp.right_shift(lookup[v * 8 : (v + 1) * 8, :], 7) for v in range(2)]

    def interpolate(source, spot, number, acc):
        acc = list(acc)
        for c in range(CAP):
            hit = [blk[v] == number * CAP + c for v in range(2)]
            for f in range(FIELDS):
                row = jnp.broadcast_to(source[spot, c * FIELDS + f : c * FIELDS + f + 1, :], (8, LANES))
                for v in range(2):
                    acc[f * 2 + v] = jnp.where(hit[v], lane_gather(row, lo[v]), acc[f * 2 + v])
        return acc

    acc = tuple(jnp.zeros((8, LANES), F32) for _ in range(12))
    acc = interpolate(block_out, me, me, acc)
    for number, _, other in [peers[i] for i in (8, 0, 1, 2, 3, 4, 5, 6, 7)]:
        pltpu.make_async_remote_copy(
            src_ref=block_out.at[number],
            dst_ref=block_in.at[number],
            send_sem=block_send.at[number],
            recv_sem=block_recv.at[number],
            device_id=other,
            device_id_type=MESH,
        ).wait_recv()
        acc = interpolate(block_in, number, number, acc)

    for f in range(FIELDS):
        both = acc[f * 2] * weight_rows[0:8, :] + acc[f * 2 + 1] * weight_rows[8:16, :]
        total = both[0:4] + both[4:8]
        if f == 4:
            total = jnp.where(front[...] == 1, ocean_temp, total)
        state[f * 4 : (f + 1) * 4, :] = total
    state[24:32, :] = jnp.zeros((8, LANES), F32)
    tiles = [state[pl.ds(h, 8, stride=4), :] for h in range(ROWS)]

    def halo_copy(k):
        return pltpu.make_async_remote_copy(
            src_ref=halo_out.at[k],
            dst_ref=ghost_in.at[k],
            send_sem=halo_send.at[k],
            recv_sem=halo_recv.at[k],
            device_id=sides[k],
            device_id_type=MESH,
        )

    for k in range(SIDES):
        for r in range(2):
            idx = jnp.broadcast_to(halo_idx[k * 2 + r : k * 2 + r + 1, :], (8, LANES))
            low = jnp.bitwise_and(idx, LANES - 1)
            high = jnp.right_shift(idx, 7)
            kept = jnp.zeros((8, LANES), F32)
            for h in range(ROWS):
                kept = jnp.where(high == h, lane_gather(tiles[h], low), kept)
            halo_out[k, :, r * LANES : (r + 1) * LANES] = kept
    for k in range(SIDES):
        halo_copy(k).start()

    out[0:24, :] = state[0:24, :]

    def look_up(rows, first):
        for t in range(SPOTS // 8):
            at = slice(t * 8, (t + 1) * 8)
            low = jnp.bitwise_and(spot_idx[at, :], LANES - 1)
            high = jnp.right_shift(spot_idx[at, :], 7)
            found = [jnp.zeros((8, LANES), F32) if first else values[f, at, :] for f in range(FIELDS)]
            for code, fetch in rows:
                hit = high == code
                for f in range(FIELDS):
                    row = jnp.broadcast_to(fetch(f), (8, LANES))
                    found[f] = jnp.where(hit, lane_gather(row, low), found[f])
            for f in range(FIELDS):
                values[f, at, :] = found[f]

    look_up([(h, lambda f, h=h: state[f * 4 + h : f * 4 + h + 1, :]) for h in range(ROWS)], True)

    for peer in peers:
        block_copy(*peer).wait_send()

    low_x, high_x = x > 0, x < count_x - 1
    low_y, high_y = y > 0, y < count_y - 1
    ghost_live = [low_x, high_x, low_y, high_y]
    back_live = [high_x, low_x, high_y, low_y]
    for k in (4, 0, 1, 2, 3):
        ghost_rows = []
        for r in range(2):
            code = jnp.where(ghost_live[k], 4 + 2 * k + r, -1) if k < 4 else 4 + 2 * (5 - layer) + r
            ghost_rows.append((code, lambda f, k=k, r=r: ghost_in[k, f : f + 1, r * LANES : (r + 1) * LANES]))
        halo_copy(k).wait_recv()
        look_up(ghost_rows, False)

    def add_sums(acc, first, last):
        for s in range(first, last):
            high = jnp.right_shift(jnp.broadcast_to(spot_idx[s : s + 1, :], (8, LANES)), 7)
            hits = [high == sub + 8 * m for m in range(2)]
            parts = [split_two(jnp.broadcast_to(contrib[c, s : s + 1, :], (8, LANES))) for c in range(4)]
            rows = [jnp.where(hits[m], parts[c][p], 0.0) for p in range(2) for c in range(4) for m in range(2)]
            left[:, s * LANES : (s + 1) * LANES] = jnp.concatenate(rows, axis=0).astype(BF16)
        at = slice(first * LANES, last * LANES)
        return acc + lax.dot_general(
            left[:, at], one_hot[:, at], (((1,), (1,)), ((), ())), preferred_element_type=F32
        )

    acc = jnp.zeros((LANES, LANES), F32)
    for r0, r1 in ((0, 0), (8, 8), (12, 16)):
        val = [[values[f, a * 20 + r0 : a * 20 + r0 + 8, :] for a in range(4)] for f in range(FIELDS)]
        grad = [[grads[(3 * a + j) * 20 + r0 : (3 * a + j) * 20 + r0 + 8, :] for j in range(3)] for a in range(4)]
        vol = vol_rows[r0 : r0 + 8, :]
        vg = [[sum(val[i][a] * grad[a][j] for a in range(4)) for j in range(3)] for i in range(3)]
        strain = [[0.5 * (vg[i][j] + vg[j][i]) for j in range(3)] for i in range(3)]
        second = 0.5 * sum(strain[i][j] * strain[i][j] for i in range(3) for j in range(3))
        pm, tm, dm = [0.25 * (val[f][0] + val[f][1] + val[f][2] + val[f][3]) for f in (3, 4, 5)]
        visc2 = (1.0 - dm) * jnp.exp(-tm) * jnp.exp(jnp.log(second + strain_reg) * (-1.0 / 3.0))
        stress = [[visc2 * strain[i][j] - (pm if i == j else 0.0) for j in range(3)] for i in range(3)]
        cont = 0.25 * vol * (vg[0][0] + vg[1][1] + vg[2][2])
        for a in range(4):
            for c in range(4):
                if c < 3:
                    part = vol * sum(stress[c][j] * grad[a][j] for j in range(3))
                    if c == 2:
                        part = part + 0.25 * gravity * vol
                else:
                    part = cont
                contrib[c, a * 20 + r0 : a * 20 + r0 + 8, :] = part
        for a in range(4):
            acc = add_sums(acc, a * 20 + r1, a * 20 + r0 + 8)

    sums[...] = acc[0:64] + acc[64:128]

    def ret_copy(k):
        return pltpu.make_async_remote_copy(
            src_ref=ret_out.at[k],
            dst_ref=ret_in.at[k],
            send_sem=ret_send.at[k],
            recv_sem=ret_recv.at[k],
            device_id=backs[k],
            device_id_type=MESH,
        )

    for k in range(SIDES):
        for r in range(2):
            row = 4 + 2 * k + r
            part = sums[pl.ds(row, 4, stride=16), :]
            if k == 4:
                part = jnp.where(layer == 0, sums[pl.ds(row + 2, 4, stride=16), :], part)
            ret_out[k, r * 4 : (r + 1) * 4, :] = part
    for k in range(SIDES):
        ret_copy(k).start()
    for k in range(SIDES):
        halo_copy(k).wait_send()

    for k in range(SIDES):
        ret_copy(k).wait_recv()
        for r in range(2):
            u = k * 2 + r
            high = jnp.right_shift(jnp.broadcast_to(halo_idx[u : u + 1, :], (8, LANES)), 7) - half
            if k < 4:
                high = jnp.where(back_live[k], high, -2)
            four = ret_in[k, r * 4 : (r + 1) * 4, :]
            parts = split_two(jnp.concatenate([four, four], axis=0))
            rows = [jnp.where(high == 2 * m, part, 0.0) for part in parts for m in range(2)]
            left_back[:, u * LANES : (u + 1) * LANES] = jnp.concatenate(rows, axis=0).astype(BF16)
    back = lax.dot_general(left_back[...], halo_hot[...], (((1,), (1,)), ((), ())), preferred_element_type=F32)
    back = back[0:16] + back[16:32]
    for h in range(ROWS):
        out[24 + h * 4 : 28 + h * 4, :] = sums[pl.ds(h, 4, stride=16), :] + back[h * 4 : (h + 1) * 4]

    for k in range(SIDES):
        ret_copy(k).wait_send()


def write_outputs(both, out_new, out_res):
    out_new[...] = both[0:24, :]
    out_res[...] = both[24:40, :]


def per_device(old_state, send_blocks, node_slots, node_weights, front_mask, halo_lists, elem_nodes, shape_grads, elem_volume):
    count_x = lax.axis_size("mapx")
    count_y = lax.axis_size("mapy")
    vmem = pl.BlockSpec(memory_space=pltpu.VMEM)
    far_memory = pl.BlockSpec(memory_space=pltpu.HBM)
    dma = pltpu.SemaphoreType.DMA
    both = pl.pallas_call(
        functools.partial(kernel, count_x, count_y),
        out_shape=jax.ShapeDtypeStruct((40, LANES), F32),
        in_specs=[far_memory] * 9,
        out_specs=vmem,
        scratch_shapes=[
            pltpu.SMEM((10, 1, CAP), jnp.int32),
            pltpu.VMEM((FIELDS * 64, LANES), F32),
            pltpu.VMEM((4, 512), jnp.int32),
            pltpu.VMEM((4, 512), F32),
            pltpu.VMEM((ROWS, LANES), jnp.int32),
            pltpu.VMEM((6, 2, LANES), jnp.int32),
            pltpu.VMEM((4, 2560), jnp.int32),
            pltpu.VMEM((240, LANES), F32),
            pltpu.VMEM((5, 4, LANES), F32),
            pltpu.VMEM((10, CAP * FIELDS, LANES), F32),
            pltpu.VMEM((10, CAP * FIELDS, LANES), F32),
            pltpu.VMEM((16, LANES), jnp.int32),
            pltpu.VMEM((16, LANES), F32),
            pltpu.VMEM((32, LANES), F32),
            pltpu.VMEM((16, LANES), jnp.int32),
            pltpu.VMEM((SIDES, 8, WIDE), F32),
            pltpu.VMEM((SIDES, 8, WIDE), F32),
            pltpu.VMEM((SPOTS, LANES), jnp.int32),
            pltpu.VMEM((LANES, SPOTS * LANES), BF16),
            pltpu.VMEM((LANES, SIDES * WIDE), BF16),
            pltpu.VMEM((FIELDS, SPOTS, LANES), F32),
            pltpu.VMEM((24, LANES), F32),
            pltpu.VMEM((4, SPOTS, LANES), F32),
            pltpu.VMEM((LANES, SPOTS * LANES), BF16),
            pltpu.VMEM((32, SIDES * WIDE), BF16),
            pltpu.VMEM((64, LANES), F32),
            pltpu.VMEM((SIDES, 8, LANES), F32),
            pltpu.VMEM((SIDES, 8, LANES), F32),
            dma((9,)),
            dma((10,)),
            dma((10,)),
            dma((SIDES,)),
            dma((SIDES,)),
            dma((SIDES,)),
            dma((SIDES,)),
        ],
        compiler_params=pltpu.CompilerParams(collective_id=0, has_side_effects=True, vmem_limit_bytes=24 << 20),
        name="remap_residual",
    )(
        *(
            pltpu.with_memory_space_constraint(value, pltpu.HBM)
            for value in (
                send_blocks.reshape(10, 1, CAP),
                old_state.reshape(FIELDS * 64, LANES),
                node_slots.reshape(4, 512),
                node_weights.reshape(4, 512),
                front_mask.reshape(ROWS, LANES),
                halo_lists.reshape(6, 2, LANES),
                elem_nodes.reshape(4, 2560),
                shape_grads.reshape(240, LANES),
                elem_volume.reshape(5, 4, LANES),
            )
        )
    )
    new_state, residual = pl.pallas_call(
        write_outputs,
        out_shape=(jax.ShapeDtypeStruct((24, LANES), F32), jax.ShapeDtypeStruct((16, LANES), F32)),
        in_specs=[vmem],
        out_specs=(vmem, vmem),
        compiler_params=pltpu.CompilerParams(vmem_limit_bytes=1 << 20),
        name="write_outputs",
    )(both)
    residual = residual.reshape(ROWS, 4, LANES).transpose(1, 0, 2)
    return new_state.reshape(1, 1, 1, FIELDS, 512), residual.reshape(1, 1, 1, 4, 512)


def solution(mesh):
    deep = P("mapx", "mapy", "layer", None, None)
    flat = P("mapx", "mapy", "layer", None)
    return jax.shard_map(
        per_device,
        mesh=mesh,
        in_specs=(deep, deep, deep, deep, flat, deep, deep, deep, flat),
        out_specs=(deep, deep),
        check_vma=False,
    )
```
